256 devices in a mesh: mem: 64 (over x, z, core), blk: 4 (over y).
Axes of the slice: x: 4, y: 4, z: 8, core: 2. Of those that a mesh axis runs over, the one named last changes fastest.
Arguments:
- ensemble: bfloat16 [128, 1048576], P('mem', 'blk'), may hold values from -6 to 6
- obs_cell: int32 [4, 512, 256], P('blk', 'mem'), may hold values from 0 to 511
- obs_count: int32 [4, 512], P('blk', 'mem'), may hold values from 1 to 256, 81920 in all within a row
- obs_value: float32 [4, 512, 256], P('blk', 'mem'), may hold values from -6 to 6
- obs_rinv: float32 [4, 512, 256], P('blk', 'mem'), may hold values from 0.05 to 0.5
Outputs:
- increments: bfloat16 [128, 1048576], P('mem', 'blk')
The draws below stay inside these ranges and needn't reach their ends.
Inputs may be any that keep to these rules, and one draw needn't show every extreme that they name: `obs_cell`: slots at or past the block's count are unused. `obs_count`: the counts of one band sum to 81920, and some block holds exactly 256.
All inputs are finite; a program needn't handle non-finite values. Where the reference program divides by a largest or mean magnitude, that divisor is 1e-20 or more.
Results may differ from the reference program's by a relative error of at most 0.0051.
Values may be sent and summed in bfloat16 or wider, within the bound.
No kernel may reach another device: no remote copies, remote signals or barrier semaphores. Data moves between devices by JAX's collectives and lax.ppermute only.
A program may use at most 64 MiB of HBM per device.

```python
import math
import jax
import jax.numpy as jnp
import numpy as np
from jax import lax

K = 128
CELLS = 512
OMAX = 256
NS_ITERS = 4
NSB = 512
CELLS_ALL = 1048576
N_BLK = 4


def place_ends(array, key, least, top_value):
    shape = array.shape
    index_at = [jax.random.randint(jax.random.fold_in(key, axis), (), 0, shape[axis]) for axis in range(len(shape))]
    array = array.at[tuple(index_at)].set(least)
    longest = shape.index(max(shape))
    index_at[longest] = (index_at[longest] + 1) % shape[longest]
    return array.at[tuple(index_at)].set(top_value)


def block_scale(key, dims, pieces, smallest, largest):
    loudness, own = 1.0, jax.random.fold_in(key, 6)
    for dim, blocks in pieces:
        draws = jnp.exp(jax.random.uniform(jax.random.fold_in(own, dim), (blocks,), jnp.float32, smallest / len(pieces), largest / len(pieces)))
        loudness = loudness * jnp.repeat(draws, dims[dim] // blocks).reshape([-1 if axis == dim else 1 for axis in range(len(dims))])
    return loudness


def length_profile(count, total, limit, lean):
    portions = [(1 << 20) // math.isqrt(grade ** lean) + 1 for grade in range(2, count + 1)]
    rest, counts = total - limit - (count - 1), [1] * (count - 1)
    while rest > 0:
        movable = [i for i in range(count - 1) if counts[i] < limit]
        mass, remaining = sum([portions[i] for i in movable]), rest
        for i in movable:
            extra = min(limit - counts[i], max(1, remaining * portions[i] // mass), rest)
            counts[i] = counts[i] + extra
            rest = rest - extra
    return np.array([limit] + counts)


def uneven(stream_key, count, total, most, lean):
    if count == 2:
        one = jax.random.randint(stream_key, (), max(1, total - most), min(most, total - 1) + 1)
        return jnp.stack([one, total - one])
    sizes = jnp.asarray(length_profile(count, total, most, lean), jnp.int32)
    pairs = (count - 1) // 2
    giver, receiver = sizes[1:1 + 2 * pairs:2], sizes[2:2 + 2 * pairs:2]
    margin = jnp.minimum(giver - 1, most - receiver)
    passed = jax.random.randint(jax.random.fold_in(stream_key, 1), (pairs,), 0, 1 << 20) % (margin + 1)
    sizes = sizes.at[1:1 + 2 * pairs:2].set(giver - passed).at[2:2 + 2 * pairs:2].set(receiver + passed)
    return sizes[jax.random.permutation(jax.random.fold_in(stream_key, 2), count)]


def bell_draw(own_key, shape, scale, bound, split=(), kind=jnp.bfloat16):
    array = jax.random.normal(own_key, shape, jnp.float32) * scale
    if len(split) > 0:
        array = block_scale(own_key, shape, split, -0.22, 0.18) * array
    return jnp.clip(array, min=-bound, max=bound).astype(kind)


def setup_inputs(seed: int = 0) -> dict:
    seeds = jax.random.split(jax.random.key(seed), 6)
    ensemble = bell_draw(seeds[0], (K, CELLS_ALL), 1.0, 6.0, ((0, 64), (1, 4)))
    obs_cell = place_ends(jax.random.randint(seeds[1], (N_BLK, NSB, OMAX), 0, CELLS), jax.random.fold_in(seeds[1], 1), 0, CELLS - 1).astype(jnp.int32)
    obs_count = jax.vmap(lambda own: uneven(own, NSB, NSB * OMAX * 5 // 8, OMAX, 2))(jax.random.split(seeds[2], N_BLK)).reshape((N_BLK, NSB)).astype(jnp.int32)
    obs_value = bell_draw(seeds[3], (N_BLK, NSB, OMAX), 1.0, 6.0, ((0, 4), (1, 64)), jnp.float32)
    obs_rinv = jnp.clip(jnp.exp(math.log(0.5) - 2.3025851 * jax.random.uniform(seeds[4], (N_BLK, NSB, OMAX), jnp.float32) ** block_scale(seeds[4], (N_BLK, NSB, OMAX), ((0, 4), (1, 64)), -0.2, 0.2)), 0.05, 0.5)
    return {"ensemble": ensemble, "obs_cell": obs_cell, "obs_count": obs_count, "obs_value": obs_value, "obs_rinv": obs_rinv}


localize = 0.5
inflation = 1.1

def center(members):
    values = members.astype(jnp.float32)
    average = lax.optimization_barrier(jnp.mean(values, axis=0))
    return (values - average[None], average)

def observe(deviation, average, cell_ids, live_counts, obs_values, inv_var):
    ensemble_size = deviation.shape[0]
    index = jnp.broadcast_to(cell_ids[None].astype(jnp.int32), (ensemble_size,) + cell_ids.shape)
    sampled = jnp.take_along_axis(deviation, index, axis=2)
    obs_mean = jnp.take_along_axis(average, cell_ids.astype(jnp.int32), axis=1)
    slots = lax.broadcasted_iota(jnp.int32, cell_ids.shape, 1)
    live = (slots < live_counts[:, None].astype(jnp.int32)).astype(jnp.float32)
    weight_root = live * jnp.sqrt(inv_var)
    upper = jnp.transpose(sampled * weight_root[None], (1, 0, 2))
    lower = (weight_root * (obs_values - obs_mean))[:, None, :]
    return jnp.concatenate([upper, lower], axis=1).astype(jnp.bfloat16)

def batch_mm(left, right):
    return jnp.einsum('bij,bjk->bik', left, right, precision=lax.Precision.HIGHEST)

def transform_apply(localized, deviation):
    ensemble_size = deviation.shape[0]
    identity = jnp.eye(ensemble_size, dtype=jnp.float32)
    system = (ensemble_size - 1) / inflation * identity + localized[:, :ensemble_size, :ensemble_size]
    forcing = localized[:, :ensemble_size, ensemble_size]
    bound_norm = lax.optimization_barrier(jnp.max(lax.optimization_barrier(jnp.sum(jnp.abs(system), axis=2)), axis=1))
    approx_y = system / bound_norm[:, None, None]
    approx_z = jnp.broadcast_to(identity, system.shape)
    for iteration in range(NS_ITERS):
        update = 1.5 * identity - 0.5 * batch_mm(approx_z, approx_y)
        approx_y = batch_mm(approx_y, update)
        approx_z = batch_mm(update, approx_z)
    root_inv = approx_z / jnp.sqrt(bound_norm)[:, None, None]
    inner = jnp.einsum('bij,bj->bi', root_inv, forcing, precision=lax.Precision.HIGHEST)
    mean_weights = jnp.einsum('bij,bj->bi', root_inv, inner, precision=lax.Precision.HIGHEST)
    mixing = jnp.sqrt(jnp.float32(ensemble_size - 1)) * root_inv + mean_weights[:, :, None] - identity
    increment = jnp.einsum('jbc,bjk->kbc', deviation, mixing, precision=lax.Precision.HIGHEST)
    return increment.astype(jnp.bfloat16)

def reference(ensemble, obs_cell, obs_count, obs_value, obs_rinv):
    bands = obs_cell.shape[0]
    sectors = obs_cell.shape[1]
    grid = jnp.transpose(ensemble.reshape(K, bands, sectors, CELLS), (1, 0, 2, 3))

    def one_band(band_inputs):
        members, cell_ids, live_counts, obs_values, inv_var = band_inputs
        deviation, average = center(members)
        obs_rows = observe(deviation, average, cell_ids, live_counts, obs_values, inv_var)
        wide_rows = obs_rows.astype(jnp.float32)
        gram_blocks = jnp.einsum('bko,bjo->bkj', wide_rows, wide_rows, precision=lax.Precision.HIGHEST)
        localized = gram_blocks + localize * (jnp.roll(gram_blocks, 1, axis=0) + jnp.roll(gram_blocks, -1, axis=0))
        return transform_apply(localized, deviation)
    result = lax.map(one_band, (grid, obs_cell, obs_count, obs_value, obs_rinv))
    return jnp.transpose(result, (1, 0, 2, 3)).reshape(K, bands * sectors * CELLS)
```

```python
import jax
import jax.numpy as jnp
from jax import lax
from jax.experimental import pallas as pl
from jax.experimental.pallas import tpu as pltpu
from jax.sharding import PartitionSpec as P

NS_ITERS = 4
localize = 0.5
inflation = 1.1

BF = jnp.bfloat16
F32 = jnp.float32
ROWS = 144


def split(a):
    high = a.astype(BF)
    return high, (a - high.astype(F32)).astype(BF)


def left_of(a):
    return jnp.concatenate(split(a), axis=1)


def right_of(a):
    pair = jnp.concatenate(split(a), axis=1)
    return jnp.concatenate([pair, pair], axis=0)


def fold(wide):
    half = wide.shape[1] // 2
    return wide[:, :half] + wide[:, half:]


def dot(a, b):
    return jnp.dot(a, b, preferred_element_type=F32)


def mm(left, right):
    return fold(dot(left, right))


def members_of(x_ref, b, width):
    piece = x_ref[:, :, b * width : (b + 1) * width]
    return piece.reshape(piece.shape[0] * piece.shape[1], width)


def centre(members):
    values = members.astype(F32)
    return values, jnp.sum(values, axis=0, keepdims=True) * (1.0 / members.shape[0])


def rows_of(members, average, cells, count, obs_value, obs_rinv):
    width, slots = members.shape[1], cells.shape[1]
    high = average.astype(BF).astype(F32)
    rest = average - high
    middle = rest.astype(BF).astype(F32)
    low = rest - middle
    line = lax.broadcasted_iota(jnp.int32, (16, width), 0)
    pieces = jnp.where(line == 0, high, jnp.where(line == 1, middle, jnp.where(line == 2, low, 0.0)))
    stacked = jnp.concatenate([members, pieces.astype(BF)], axis=0)
    position = lax.broadcasted_iota(jnp.int32, (width, slots), 0)
    selector = jnp.where(position == cells, 1.0, 0.0).astype(BF)
    sampled = dot(stacked, selector)
    size = members.shape[0]
    mean_at = jnp.sum(sampled[size:], axis=0, keepdims=True)
    slot = lax.broadcasted_iota(jnp.int32, (1, slots), 1)
    root = jnp.where(slot < count, jnp.sqrt(obs_rinv), 0.0)
    upper = (sampled[:size] - mean_at) * root
    lower = root * (obs_value - mean_at)
    line = lax.broadcasted_iota(jnp.int32, (ROWS - size, slots), 0)
    lower = jnp.where(line == 0, lower, 0.0)
    return jnp.concatenate([upper, lower], axis=0).astype(BF)


def gram_of(rows):
    return lax.dot_general(rows, rows[:128], (((1,), (1,)), ((), ())), preferred_element_type=F32)


def eye_of(size):
    i = lax.broadcasted_iota(jnp.int32, (size, size), 0)
    j = lax.broadcasted_iota(jnp.int32, (size, size), 1)
    return jnp.where(i == j, 1.0, 0.0).astype(F32)


def transforms(localized, eye):
    size = eye.shape[0]
    systems = [g[:size] + (size - 1) / inflation * eye for g in localized]
    forcings = [g[size : size + 1] for g in localized]
    bounds = [
        jnp.max(jnp.sum(jnp.abs(a), axis=0, keepdims=True), axis=1, keepdims=True) for a in systems
    ]
    scales = [1.0 / b for b in bounds]
    y = [a * s for a, s in zip(systems, scales)]
    u = [1.5 * eye - 0.5 * a for a in y]
    z = u
    y = [mm(left_of(a), right_of(b)) for a, b in zip(y, u)]
    for iteration in range(NS_ITERS - 1):
        u = [1.5 * eye - 0.5 * mm(left_of(a), right_of(b)) for a, b in zip(z, y)]
        if iteration < NS_ITERS - 2:
            both = [
                mm(jnp.concatenate([left_of(a), left_of(c)], axis=0), right_of(b))
                for a, c, b in zip(y, z, u)
            ]
            y = [a[:size] for a in both]
            z = [a[size:] for a in both]
        else:
            z = [mm(left_of(a), right_of(b)) for a, b in zip(z, u)]
    out = []
    for a, f, s in zip(z, forcings, scales):
        inner = jnp.sum(a * f, axis=1, keepdims=True)
        weights = jnp.sum(a * inner, axis=0, keepdims=True) * s
        out.append(jnp.sqrt(s * (size - 1.0)) * a + weights - eye)
    return out


def apply_to(transform, values, average):
    high, low = split(values - average)
    t_high, t_low = split(transform)
    increment = dot(jnp.concatenate([t_high, t_low], axis=1), jnp.concatenate([high, high], axis=0))
    return (increment + dot(t_high, low)).astype(BF)


def boundary_rows_kernel(blocks, x_ref, cell_ref, count_ref, value_ref, rinv_ref, first_ref, last_ref):
    width = x_ref.shape[2] // blocks
    for b, out_ref in ((0, first_ref), (blocks - 1, last_ref)):
        members = members_of(x_ref, b, width)
        _, average = centre(members)
        out_ref[...] = rows_of(
            members, average, cell_ref[b : b + 1], count_ref[0, b], value_ref[b : b + 1], rinv_ref[b : b + 1]
        )


def interior_kernel(
    blocks, x_ref, cell_ref, count_ref, value_ref, rinv_ref, first_ref, last_ref, out_ref, part_ref
):
    width = x_ref.shape[2] // blocks
    inner = range(1, blocks - 1)
    values, averages, grams = {}, {}, {}
    grams[0] = gram_of(first_ref[...])
    grams[blocks - 1] = gram_of(last_ref[...])
    for b in inner:
        members = members_of(x_ref, b, width)
        _, average = centre(members)
        grams[b] = gram_of(
            rows_of(members, average, cell_ref[b : b + 1], count_ref[0, b], value_ref[b : b + 1], rinv_ref[b : b + 1])
        )
    part_ref[0] = grams[0] + localize * grams[1]
    part_ref[1] = grams[blocks - 1] + localize * grams[blocks - 2]
    eye = eye_of(128)
    mixed = transforms([grams[b] + localize * (grams[b - 1] + grams[b + 1]) for b in inner], eye)
    for b, transform in zip(inner, mixed):
        values, average = centre(members_of(x_ref, b, width))
        result = apply_to(transform, values, average)
        out_ref[:, :, (b - 1) * width : b * width] = result.reshape(x_ref.shape[0], x_ref.shape[1], width)


def boundary_kernel(blocks, x_ref, part_ref, left_ref, right_ref, in_ref, out_ref):
    width = x_ref.shape[2] // blocks
    out_ref[:, :, width : (blocks - 1) * width] = in_ref[...]
    eye = eye_of(128)
    localized = [
        part_ref[0] + localize * gram_of(left_ref[...]),
        part_ref[1] + localize * gram_of(right_ref[...]),
    ]
    for b, transform in zip((0, blocks - 1), transforms(localized, eye)):
        values, average = centre(members_of(x_ref, b, width))
        result = apply_to(transform, values, average)
        out_ref[:, :, b * width : (b + 1) * width] = result.reshape(x_ref.shape[0], x_ref.shape[1], width)


VMEM = pl.BlockSpec(memory_space=pltpu.VMEM)
SMEM = pl.BlockSpec(memory_space=pltpu.SMEM)


def call(kernel, out_shape, args, specs, flops):
    outs = jax.tree.map(lambda _: VMEM, out_shape)
    moved = sum(a.size * a.dtype.itemsize for a in args)
    return pl.pallas_call(
        kernel,
        out_shape=out_shape,
        in_specs=specs,
        out_specs=outs,
        cost_estimate=pl.CostEstimate(flops=flops, bytes_accessed=moved, transcendentals=0),
        compiler_params=pltpu.CompilerParams(vmem_limit_bytes=40 * 2**20),
    )(*args)


def analyse(arrived, cells, counts, obs_value, obs_rinv, exchange):
    blocks, slots = cells.shape
    kernel = lambda body: (lambda *refs: body(blocks, *refs))
    rows = jax.ShapeDtypeStruct((ROWS, slots), BF)
    obs = (cells, counts, obs_value, obs_rinv)
    specs = [VMEM, VMEM, SMEM, VMEM, VMEM]
    first, last = call(kernel(boundary_rows_kernel), (rows, rows), (arrived,) + obs, specs, 2 * 10**8)
    left, right = exchange(first, last)
    part = jax.ShapeDtypeStruct((2, ROWS, 128), F32)
    out = jax.ShapeDtypeStruct(arrived.shape[:2] + (arrived.shape[2] // blocks * (blocks - 2),), BF)
    out, part = call(
        kernel(interior_kernel), (out, part), (arrived,) + obs + (first, last), specs + [VMEM, VMEM], 5 * 10**9
    )
    return call(
        kernel(boundary_kernel), jax.ShapeDtypeStruct(arrived.shape, BF), (arrived, part, left, right, out),
        [VMEM] * 5, 2 * 10**9,
    )


def neighbours(first, last):
    count = lax.axis_size("mem")
    forward = [(i, (i + 1) % count) for i in range(count)]
    backward = [(target, source) for source, target in forward]
    return lax.ppermute(last, "mem", forward), lax.ppermute(first, "mem", backward)


def on_device(ensemble, obs_cell, obs_count, obs_value, obs_rinv):
    groups = lax.axis_size("mem")
    local = ensemble.shape[0]
    pieces = ensemble.reshape(local, groups, -1).transpose(1, 0, 2)
    arrived = lax.all_to_all(pieces, "mem", split_axis=0, concat_axis=0, tiled=True)
    outgoing = analyse(arrived, obs_cell[0], obs_count, obs_value[0], obs_rinv[0], neighbours)
    returned = lax.all_to_all(outgoing, "mem", split_axis=0, concat_axis=0, tiled=True)
    return returned.transpose(1, 0, 2).reshape(ensemble.shape)


def solution(mesh):
    placed = (
        P("mem", "blk"),
        P("blk", "mem", None),
        P("blk", "mem"),
        P("blk", "mem", None),
        P("blk", "mem", None),
    )
    return jax.shard_map(
        on_device, mesh=mesh, in_specs=placed, out_specs=P("mem", "blk"), check_vma=False
    )
```

```python
import jax
import jax.numpy as jnp
from jax import lax
from jax.experimental import pallas as pl
from jax.experimental.pallas import tpu as pltpu
from jax.sharding import PartitionSpec as P

NS_ITERS = 4
localize = 0.5
inflation = 1.1

BF = jnp.bfloat16
F32 = jnp.float32
ROWS = 144


def split(a):
    high = a.astype(BF)
    return high, (a - high.astype(F32)).astype(BF)


def left_of(a):
    return jnp.concatenate(split(a), axis=1)


def right_of(a):
    pair = jnp.concatenate(split(a), axis=1)
    return jnp.concatenate([pair, pair], axis=0)


def fold(wide):
    half = wide.shape[1] // 2
    return wide[:, :half] + wide[:, half:]


def dot(a, b):
    return jnp.dot(a, b, preferred_element_type=F32)


def mm(left, right):
    return fold(dot(left, right))


def members_of(x_ref, b, width):
    piece = x_ref[:, :, b * width : (b + 1) * width]
    return piece.reshape(piece.shape[0] * piece.shape[1], width)


def centre(members):
    values = members.astype(F32)
    return values, jnp.sum(values, axis=0, keepdims=True) * (1.0 / members.shape[0])


def rows_of(members, average, cells, count, obs_value, obs_rinv):
    width, slots = members.shape[1], cells.shape[1]
    high = average.astype(BF).astype(F32)
    rest = average - high
    middle = rest.astype(BF).astype(F32)
    low = rest - middle
    line = lax.broadcasted_iota(jnp.int32, (16, width), 0)
    pieces = jnp.where(line == 0, high, jnp.where(line == 1, middle, jnp.where(line == 2, low, 0.0)))
    stacked = jnp.concatenate([members, pieces.astype(BF)], axis=0)
    position = lax.broadcasted_iota(jnp.int32, (width, slots), 0)
    selector = jnp.where(position == cells, 1.0, 0.0).astype(BF)
    sampled = dot(stacked, selector)
    size = members.shape[0]
    mean_at = jnp.sum(sampled[size:], axis=0, keepdims=True)
    slot = lax.broadcasted_iota(jnp.int32, (1, slots), 1)
    root = jnp.where(slot < count, jnp.sqrt(obs_rinv), 0.0)
    upper = (sampled[:size] - mean_at) * root
    lower = root * (obs_value - mean_at)
    line = lax.broadcasted_iota(jnp.int32, (ROWS - size, slots), 0)
    lower = jnp.where(line == 0, lower, 0.0)
    return jnp.concatenate([upper, lower], axis=0).astype(BF)


def gram_of(rows):
    return lax.dot_general(rows, rows[:128], (((1,), (1,)), ((), ())), preferred_element_type=F32)


def eye_of(size):
    i = lax.broadcasted_iota(jnp.int32, (size, size), 0)
    j = lax.broadcasted_iota(jnp.int32, (size, size), 1)
    return jnp.where(i == j, 1.0, 0.0).astype(F32)


def transforms(localized, eye):
    size = eye.shape[0]
    systems = [g[:size] + (size - 1) / inflation * eye for g in localized]
    forcings = [g[size : size + 1] for g in localized]
    bounds = [
        jnp.max(jnp.sum(jnp.abs(a), axis=0, keepdims=True), axis=1, keepdims=True) for a in systems
    ]
    scales = [1.0 / b for b in bounds]
    y = [a * s for a, s in zip(systems, scales)]
    u = [1.5 * eye - 0.5 * a for a in y]
    z = u
    y = [mm(left_of(a), right_of(b)) for a, b in zip(y, u)]
    for iteration in range(NS_ITERS - 1):
        u = [1.5 * eye - 0.5 * mm(left_of(a), right_of(b)) for a, b in zip(z, y)]
        if iteration < NS_ITERS - 2:
            both = [
                mm(jnp.concatenate([left_of(a), left_of(c)], axis=0), right_of(b))
                for a, c, b in zip(y, z, u)
            ]
            y = [a[:size] for a in both]
            z = [a[size:] for a in both]
        else:
            z = [mm(left_of(a), right_of(b)) for a, b in zip(z, u)]
    out = []
    for a, f, s in zip(z, forcings, scales):
        inner = jnp.sum(a * f, axis=1, keepdims=True)
        weights = jnp.sum(a * inner, axis=0, keepdims=True) * s
        out.append(jnp.sqrt(s * (size - 1.0)) * a + weights - eye)
    return out


def apply_to(transform, deviation):
    high, low = split(transform)
    increment = dot(jnp.concatenate([high, high], axis=1), deviation)
    return (increment + dot(low, deviation[:128])).astype(BF)


def block_rows(b, members, average, obs_refs):
    cell_ref, count_ref, value_ref, rinv_ref = obs_refs
    one = slice(b, b + 1)
    return rows_of(members, average, cell_ref[one], count_ref[0:1, one], value_ref[one], rinv_ref[one])


def boundary_kernel(blocks, x_ref, cell_ref, count_ref, value_ref, rinv_ref, first_ref, last_ref):
    width = x_ref.shape[2] // blocks
    for b, out_ref in ((0, first_ref), (blocks - 1, last_ref)):
        members = members_of(x_ref, b, width)
        _, average = centre(members)
        out_ref[...] = block_rows(b, members, average, (cell_ref, count_ref, value_ref, rinv_ref))


def gram_kernel(
    blocks, x_ref, cell_ref, count_ref, value_ref, rinv_ref, first_ref, last_ref, local_ref, dev_ref
):
    width = x_ref.shape[2] // blocks
    grams = []
    for b in range(blocks):
        members = members_of(x_ref, b, width)
        values, average = centre(members)
        high, low = split(values - average)
        dev_ref[b, :128] = high
        dev_ref[b, 128:] = low
        if b == 0:
            rows = first_ref[...]
        elif b == blocks - 1:
            rows = last_ref[...]
        else:
            rows = block_rows(b, members, average, (cell_ref, count_ref, value_ref, rinv_ref))
        grams.append(gram_of(rows))
        if b > 0:
            below = grams[b - 1]
            if b > 1:
                below = below + localize * grams[b - 2]
            local_ref[b - 1] = below + localize * grams[b]
    local_ref[blocks - 1] = grams[blocks - 1] + localize * grams[blocks - 2]


def analysis_kernel(blocks, local_ref, dev_ref, left_ref, right_ref, out_ref):
    width = out_ref.shape[2] // blocks
    localized = [local_ref[b] for b in range(blocks)]
    localized[0] = localized[0] + localize * gram_of(left_ref[...])
    localized[-1] = localized[-1] + localize * gram_of(right_ref[...])
    for b, transform in enumerate(transforms(localized, eye_of(128))):
        result = apply_to(transform, dev_ref[b])
        out_ref[:, :, b * width : (b + 1) * width] = result.reshape(out_ref.shape[0], out_ref.shape[1], width)


VMEM = pl.BlockSpec(memory_space=pltpu.VMEM)


def call(kernel, out_shape, args, flops):
    outs = jax.tree.map(lambda _: VMEM, out_shape)
    moved = sum(a.size * a.dtype.itemsize for a in args)
    return pl.pallas_call(
        kernel,
        out_shape=out_shape,
        in_specs=[VMEM] * len(args),
        out_specs=outs,
        cost_estimate=pl.CostEstimate(flops=flops, bytes_accessed=moved, transcendentals=0),
        compiler_params=pltpu.CompilerParams(vmem_limit_bytes=40 * 2**20),
    )(*args)


def analyse(arrived, cells, counts, obs_value, obs_rinv, exchange):
    blocks, slots = cells.shape
    kernel = lambda body: (lambda *refs: body(blocks, *refs))
    rows = jax.ShapeDtypeStruct((ROWS, slots), BF)
    obs = (cells, counts, obs_value, obs_rinv)
    first, last = call(kernel(boundary_kernel), (rows, rows), (arrived,) + obs, 2 * 10**8)
    left, right = exchange(first, last)
    localized = jax.ShapeDtypeStruct((blocks, ROWS, 128), F32)
    deviation = jax.ShapeDtypeStruct((blocks, 256, arrived.shape[2] // blocks), BF)
    localized, deviation = call(
        kernel(gram_kernel), (localized, deviation), (arrived,) + obs + (first, last), 5 * 10**9
    )
    return call(
        kernel(analysis_kernel), jax.ShapeDtypeStruct(arrived.shape, BF), (localized, deviation, left, right), 5 * 10**9
    )


def neighbours(first, last):
    count = lax.axis_size("mem")
    forward = [(i, (i + 1) % count) for i in range(count)]
    backward = [(target, source) for source, target in forward]
    return lax.ppermute(last, "mem", forward), lax.ppermute(first, "mem", backward)


def on_device(ensemble, obs_cell, obs_count, obs_value, obs_rinv):
    groups = lax.axis_size("mem")
    local, cells = ensemble.shape
    arrived = lax.all_to_all(ensemble, "mem", split_axis=1, concat_axis=1, tiled=True)
    arrived = arrived.reshape(local, groups, cells // groups).transpose(1, 0, 2)
    outgoing = analyse(arrived, obs_cell[0], obs_count, obs_value[0], obs_rinv[0], neighbours)
    outgoing = outgoing.transpose(1, 0, 2).reshape(local, cells)
    return lax.all_to_all(outgoing, "mem", split_axis=1, concat_axis=1, tiled=True)


def solution(mesh):
    placed = (
        P("mem", "blk"),
        P("blk", "mem", None),
        P("blk", "mem"),
        P("blk", "mem", None),
        P("blk", "mem", None),
    )
    return jax.shard_map(
        on_device, mesh=mesh, in_specs=placed, out_specs=P("mem", "blk"), check_vma=False
    )
```

```python
import jax
import jax.numpy as jnp
from jax import lax
from jax.experimental import pallas as pl
from jax.experimental.pallas import tpu as pltpu
from jax.sharding import PartitionSpec as P

NS_ITERS = 4
localize = 0.5
inflation = 1.1

BF = jnp.bfloat16
F32 = jnp.float32
ROWS = 144


def split(a):
    high = a.astype(BF)
    return high, (a - high.astype(F32)).astype(BF)


def left_of(a):
    return jnp.concatenate(split(a), axis=1)


def right_of(a):
    pair = jnp.concatenate(split(a), axis=1)
    return jnp.concatenate([pair, pair], axis=0)


def fold(wide):
    half = wide.shape[1] // 2
    return wide[:, :half] + wide[:, half:]


def dot(a, b):
    return jnp.dot(a, b, preferred_element_type=F32)


def mm(left, right):
    return fold(dot(left, right))


def members_of(x_ref, b, width):
    piece = x_ref[:, :, b * width : (b + 1) * width]
    return piece.reshape(piece.shape[0] * piece.shape[1], width)


def centre(members):
    values = members.astype(F32)
    return values, jnp.sum(values, axis=0, keepdims=True) * (1.0 / members.shape[0])


def rows_of(members, average, cells, count, obs_value, obs_rinv):
    width, slots = members.shape[1], cells.shape[1]
    high = average.astype(BF).astype(F32)
    rest = average - high
    middle = rest.astype(BF).astype(F32)
    low = rest - middle
    line = lax.broadcasted_iota(jnp.int32, (16, width), 0)
    pieces = jnp.where(line == 0, high, jnp.where(line == 1, middle, jnp.where(line == 2, low, 0.0)))
    stacked = jnp.concatenate([members, pieces.astype(BF)], axis=0)
    position = lax.broadcasted_iota(jnp.int32, (width, slots), 0)
    selector = jnp.where(position == cells, 1.0, 0.0).astype(BF)
    sampled = dot(stacked, selector)
    size = members.shape[0]
    mean_at = jnp.sum(sampled[size:], axis=0, keepdims=True)
    slot = lax.broadcasted_iota(jnp.int32, (1, slots), 1)
    root = jnp.where(slot < count, jnp.sqrt(obs_rinv), 0.0)
    upper = (sampled[:size] - mean_at) * root
    lower = root * (obs_value - mean_at)
    line = lax.broadcasted_iota(jnp.int32, (ROWS - size, slots), 0)
    lower = jnp.where(line == 0, lower, 0.0)
    return jnp.concatenate([upper, lower], axis=0).astype(BF)


def gram_of(rows):
    return lax.dot_general(rows, rows[:128], (((1,), (1,)), ((), ())), preferred_element_type=F32)


def eye_of(size):
    i = lax.broadcasted_iota(jnp.int32, (size, size), 0)
    j = lax.broadcasted_iota(jnp.int32, (size, size), 1)
    return jnp.where(i == j, 1.0, 0.0).astype(F32)


def transforms(localized, eye):
    size = eye.shape[0]
    systems = [g[:size] + (size - 1) / inflation * eye for g in localized]
    forcings = [g[size : size + 1] for g in localized]
    bounds = [
        jnp.max(jnp.sum(jnp.abs(a), axis=0, keepdims=True), axis=1, keepdims=True) for a in systems
    ]
    scales = [1.0 / b for b in bounds]
    y = [a * s for a, s in zip(systems, scales)]
    u = [1.5 * eye - 0.5 * a for a in y]
    z = u
    y = [mm(left_of(a), right_of(b)) for a, b in zip(y, u)]
    for iteration in range(NS_ITERS - 1):
        u = [1.5 * eye - 0.5 * mm(left_of(a), right_of(b)) for a, b in zip(z, y)]
        if iteration < NS_ITERS - 2:
            both = [
                mm(jnp.concatenate([left_of(a), left_of(c)], axis=0), right_of(b))
                for a, c, b in zip(y, z, u)
            ]
            y = [a[:size] for a in both]
            z = [a[size:] for a in both]
        else:
            z = [mm(left_of(a), right_of(b)) for a, b in zip(z, u)]
    out = []
    for a, f, s in zip(z, forcings, scales):
        inner = jnp.sum(a * f, axis=1, keepdims=True)
        weights = jnp.sum(a * inner, axis=0, keepdims=True) * s
        out.append(jnp.sqrt(s * (size - 1.0)) * a + weights - eye)
    return out


def apply_to(transform, deviation):
    high, low = split(transform)
    increment = dot(jnp.concatenate([high, high], axis=1), deviation)
    return (increment + dot(low, deviation[:128])).astype(BF)


def block_rows(b, members, average, obs_refs):
    cell_ref, count_ref, value_ref, rinv_ref = obs_refs
    one = slice(b, b + 1)
    return rows_of(members, average, cell_ref[one], count_ref[0:1, one], value_ref[one], rinv_ref[one])


def is_even():
    return lax.rem(lax.axis_index("mem"), 2) == 0


def boundary_kernel(blocks, x_ref, cell_ref, count_ref, value_ref, rinv_ref, across_ref, partner_ref):
    width = x_ref.shape[2] // blocks
    rows = []
    for b in (0, blocks - 1):
        members = members_of(x_ref, b, width)
        _, average = centre(members)
        rows.append(block_rows(b, members, average, (cell_ref, count_ref, value_ref, rinv_ref)))
    first, last = rows

    @pl.when(is_even())
    def _():
        across_ref[...] = first
        partner_ref[...] = last

    @pl.when(jnp.logical_not(is_even()))
    def _():
        across_ref[...] = last
        partner_ref[...] = first


def ordered(across_ref, partner_ref):
    across, partner = gram_of(across_ref[...]), gram_of(partner_ref[...])
    even = is_even()
    return jnp.where(even, across, partner), jnp.where(even, partner, across)


def gram_kernel(
    blocks, x_ref, cell_ref, count_ref, value_ref, rinv_ref, across_ref, partner_ref, local_ref, dev_ref
):
    width = x_ref.shape[2] // blocks
    first_gram, last_gram = ordered(across_ref, partner_ref)
    grams = []
    for b in range(blocks):
        members = members_of(x_ref, b, width)
        values, average = centre(members)
        high, low = split(values - average)
        dev_ref[b, :128] = high
        dev_ref[b, 128:] = low
        if b == 0:
            grams.append(first_gram)
        elif b == blocks - 1:
            grams.append(last_gram)
        else:
            grams.append(gram_of(block_rows(b, members, average, (cell_ref, count_ref, value_ref, rinv_ref))))
        if b > 0:
            below = grams[b - 1]
            if b > 1:
                below = below + localize * grams[b - 2]
            local_ref[b - 1] = below + localize * grams[b]
    local_ref[blocks - 1] = grams[blocks - 1] + localize * grams[blocks - 2]


def analysis_kernel(blocks, local_ref, dev_ref, across_ref, partner_ref, out_ref):
    width = out_ref.shape[2] // blocks
    localized = [local_ref[b] for b in range(blocks)]
    left, right = ordered(across_ref, partner_ref)
    localized[0] = localized[0] + localize * left
    localized[-1] = localized[-1] + localize * right
    for b, transform in enumerate(transforms(localized, eye_of(128))):
        result = apply_to(transform, dev_ref[b])
        out_ref[:, :, b * width : (b + 1) * width] = result.reshape(out_ref.shape[0], out_ref.shape[1], width)


VMEM = pl.BlockSpec(memory_space=pltpu.VMEM)


def call(kernel, out_shape, args, flops):
    outs = jax.tree.map(lambda _: VMEM, out_shape)
    moved = sum(a.size * a.dtype.itemsize for a in args)
    return pl.pallas_call(
        kernel,
        out_shape=out_shape,
        in_specs=[VMEM] * len(args),
        out_specs=outs,
        cost_estimate=pl.CostEstimate(flops=flops, bytes_accessed=moved, transcendentals=0),
        compiler_params=pltpu.CompilerParams(vmem_limit_bytes=40 * 2**20),
    )(*args)


def analyse(arrived, cells, counts, obs_value, obs_rinv, exchange):
    blocks, slots = cells.shape
    kernel = lambda body: (lambda *refs: body(blocks, *refs))
    rows = jax.ShapeDtypeStruct((ROWS, slots), BF)
    obs = (cells, counts, obs_value, obs_rinv)
    across, partner = call(kernel(boundary_kernel), (rows, rows), (arrived,) + obs, 2 * 10**8)
    halo = exchange(across, partner)
    localized = jax.ShapeDtypeStruct((blocks, ROWS, 128), F32)
    deviation = jax.ShapeDtypeStruct((blocks, 256, arrived.shape[2] // blocks), BF)
    localized, deviation = call(
        kernel(gram_kernel), (localized, deviation), (arrived,) + obs + (across, partner), 5 * 10**9
    )
    return call(
        kernel(analysis_kernel), jax.ShapeDtypeStruct(arrived.shape, BF), (localized, deviation) + halo, 5 * 10**9
    )


def swap_boundaries(across, partner):
    count = lax.axis_size("mem")
    hops = [(i, (i + 1) % count) for i in range(1, count, 2)]
    cores = [(i, i + 1) for i in range(0, count, 2)]
    both_ways = lambda pairs: pairs + [(target, source) for source, target in pairs]
    return lax.ppermute(across, "mem", both_ways(hops)), lax.ppermute(partner, "mem", both_ways(cores))


def on_device(ensemble, obs_cell, obs_count, obs_value, obs_rinv):
    groups = lax.axis_size("mem")
    local, cells = ensemble.shape
    arrived = lax.all_to_all(ensemble, "mem", split_axis=1, concat_axis=1, tiled=True)
    arrived = arrived.reshape(local, groups, cells // groups).transpose(1, 0, 2)
    outgoing = analyse(arrived, obs_cell[0], obs_count, obs_value[0], obs_rinv[0], swap_boundaries)
    outgoing = outgoing.transpose(1, 0, 2).reshape(local, cells)
    return lax.all_to_all(outgoing, "mem", split_axis=1, concat_axis=1, tiled=True)


def solution(mesh):
    placed = (
        P("mem", "blk"),
        P("blk", "mem", None),
        P("blk", "mem"),
        P("blk", "mem", None),
        P("blk", "mem", None),
    )
    return jax.shard_map(
        on_device, mesh=mesh, in_specs=placed, out_specs=P("mem", "blk"), check_vma=False
    )
```

```python
import jax
import jax.numpy as jnp
from jax import lax
from jax.experimental import pallas as pl
from jax.experimental.pallas import tpu as pltpu
from jax.sharding import PartitionSpec as P

NS_ITERS = 4
localize = 0.5
inflation = 1.1

BF = jnp.bfloat16
F32 = jnp.float32
ROWS = 144


def split(a):
    high = a.astype(BF)
    return high, (a - high.astype(F32)).astype(BF)


def left_of(a):
    return jnp.concatenate(split(a), axis=1)


def right_of(a):
    pair = jnp.concatenate(split(a), axis=1)
    return jnp.concatenate([pair, pair], axis=0)


def fold(wide):
    half = wide.shape[1] // 2
    return wide[:, :half] + wide[:, half:]


def dot(a, b):
    return jnp.dot(a, b, preferred_element_type=F32)


def mm(left, right):
    return fold(dot(left, right))


def members_of(x_ref, b, width):
    piece = x_ref[:, :, b * width : (b + 1) * width]
    return piece.reshape(piece.shape[0] * piece.shape[1], width)


def centre(members):
    values = members.astype(F32)
    return values, jnp.sum(values, axis=0, keepdims=True) * (1.0 / members.shape[0])


def rows_of(b, blocks, members, average, obs_ref):
    width, slots = members.shape[1], obs_ref.shape[1]
    cells = obs_ref[b : b + 1].astype(jnp.int32)
    obs_value = obs_ref[blocks + b : blocks + b + 1]
    root = obs_ref[2 * blocks + b : 2 * blocks + b + 1]
    high = average.astype(BF).astype(F32)
    rest = average - high
    middle = rest.astype(BF).astype(F32)
    low = rest - middle
    line = lax.broadcasted_iota(jnp.int32, (16, width), 0)
    pieces = jnp.where(line == 0, high, jnp.where(line == 1, middle, jnp.where(line == 2, low, 0.0)))
    stacked = jnp.concatenate([members, pieces.astype(BF)], axis=0)
    position = lax.broadcasted_iota(jnp.int32, (width, slots), 0)
    selector = jnp.where(position == cells, 1.0, 0.0).astype(BF)
    sampled = dot(stacked, selector)
    size = members.shape[0]
    mean_at = jnp.sum(sampled[size:], axis=0, keepdims=True)
    upper = (sampled[:size] - mean_at) * root
    lower = root * (obs_value - mean_at)
    line = lax.broadcasted_iota(jnp.int32, (ROWS - size, slots), 0)
    lower = jnp.where(line == 0, lower, 0.0)
    return jnp.concatenate([upper, lower], axis=0).astype(BF)


def gram_of(rows):
    return lax.dot_general(rows, rows[:128], (((1,), (1,)), ((), ())), preferred_element_type=F32)


def eye_of(size):
    i = lax.broadcasted_iota(jnp.int32, (size, size), 0)
    j = lax.broadcasted_iota(jnp.int32, (size, size), 1)
    return jnp.where(i == j, 1.0, 0.0).astype(F32)


def transforms(localized, eye):
    size = eye.shape[0]
    systems = [g[:size] + (size - 1) / inflation * eye for g in localized]
    forcings = [g[size : size + 1] for g in localized]
    bounds = [
        jnp.max(jnp.sum(jnp.abs(a), axis=0, keepdims=True), axis=1, keepdims=True) for a in systems
    ]
    scales = [1.0 / b for b in bounds]
    y = [a * s for a, s in zip(systems, scales)]
    u = [1.5 * eye - 0.5 * a for a in y]
    z = u
    y = [mm(left_of(a), right_of(b)) for a, b in zip(y, u)]
    for iteration in range(NS_ITERS - 1):
        u = [1.5 * eye - 0.5 * mm(left_of(a), right_of(b)) for a, b in zip(z, y)]
        if iteration < NS_ITERS - 2:
            both = [
                mm(jnp.concatenate([left_of(a), left_of(c)], axis=0), right_of(b))
                for a, c, b in zip(y, z, u)
            ]
            y = [a[:size] for a in both]
            z = [a[size:] for a in both]
        else:
            z = [mm(left_of(a), right_of(b)) for a, b in zip(z, u)]
    out = []
    for a, f, s in zip(z, forcings, scales):
        inner = jnp.sum(a * f, axis=1, keepdims=True)
        weights = jnp.sum(a * inner, axis=0, keepdims=True) * s
        out.append(jnp.sqrt(s * (size - 1.0)) * a + weights - eye)
    return out


def apply_to(transform, deviation):
    high, low = split(transform)
    increment = dot(jnp.concatenate([high, high], axis=1), deviation)
    return (increment + dot(low, deviation[:128])).astype(BF)


def is_even():
    return lax.rem(lax.axis_index("mem"), 2) == 0


def boundary_kernel(blocks, x_ref, obs_ref, across_ref, partner_ref):
    width = x_ref.shape[2] // blocks
    rows = []
    for b in (0, blocks - 1):
        members = members_of(x_ref, b, width)
        _, average = centre(members)
        rows.append(rows_of(b, blocks, members, average, obs_ref))
    first, last = rows

    @pl.when(is_even())
    def _():
        across_ref[...] = first
        partner_ref[...] = last

    @pl.when(jnp.logical_not(is_even()))
    def _():
        across_ref[...] = last
        partner_ref[...] = first


def ordered(across_ref, partner_ref):
    across, partner = gram_of(across_ref[...]), gram_of(partner_ref[...])
    even = is_even()
    return jnp.where(even, across, partner), jnp.where(even, partner, across)


def gram_kernel(blocks, x_ref, obs_ref, across_ref, partner_ref, local_ref, dev_ref):
    width = x_ref.shape[2] // blocks
    first_gram, last_gram = ordered(across_ref, partner_ref)
    grams = []
    for b in range(blocks):
        members = members_of(x_ref, b, width)
        values, average = centre(members)
        high, low = split(values - average)
        dev_ref[b, :128] = high
        dev_ref[b, 128:] = low
        if b == 0:
            grams.append(first_gram)
        elif b == blocks - 1:
            grams.append(last_gram)
        else:
            grams.append(gram_of(rows_of(b, blocks, members, average, obs_ref)))
        if b > 0:
            below = grams[b - 1]
            if b > 1:
                below = below + localize * grams[b - 2]
            local_ref[b - 1] = below + localize * grams[b]
    local_ref[blocks - 1] = grams[blocks - 1] + localize * grams[blocks - 2]


def analysis_kernel(blocks, local_ref, dev_ref, across_ref, partner_ref, out_ref):
    width = out_ref.shape[2] // blocks
    localized = [local_ref[b] for b in range(blocks)]
    left, right = ordered(across_ref, partner_ref)
    localized[0] = localized[0] + localize * left
    localized[-1] = localized[-1] + localize * right
    for b, transform in enumerate(transforms(localized, eye_of(128))):
        result = apply_to(transform, dev_ref[b])
        out_ref[:, :, b * width : (b + 1) * width] = result.reshape(out_ref.shape[0], out_ref.shape[1], width)


VMEM = pl.BlockSpec(memory_space=pltpu.VMEM)


def call(kernel, out_shape, args, flops):
    outs = jax.tree.map(lambda _: VMEM, out_shape)
    moved = sum(a.size * a.dtype.itemsize for a in args)
    return pl.pallas_call(
        kernel,
        out_shape=out_shape,
        in_specs=[VMEM] * len(args),
        out_specs=outs,
        cost_estimate=pl.CostEstimate(flops=flops, bytes_accessed=moved, transcendentals=0),
        compiler_params=pltpu.CompilerParams(vmem_limit_bytes=40 * 2**20),
    )(*args)


def packed(obs_cell, obs_count, obs_value, obs_rinv):
    slot = lax.broadcasted_iota(jnp.int32, obs_cell.shape, 1)
    root = jnp.where(slot < obs_count[:, None], jnp.sqrt(obs_rinv), 0.0)
    return jnp.concatenate([obs_cell.astype(F32), obs_value, root], axis=0)


def analyse(arrived, obs, exchange):
    blocks, slots = obs.shape[0] // 3, obs.shape[1]
    kernel = lambda body: (lambda *refs: body(blocks, *refs))
    rows = jax.ShapeDtypeStruct((ROWS, slots), BF)
    across, partner = call(kernel(boundary_kernel), (rows, rows), (arrived, obs), 2 * 10**8)
    halo = exchange(across, partner)
    localized = jax.ShapeDtypeStruct((blocks, ROWS, 128), F32)
    deviation = jax.ShapeDtypeStruct((blocks, 256, arrived.shape[2] // blocks), BF)
    localized, deviation = call(
        kernel(gram_kernel), (localized, deviation), (arrived, obs, across, partner), 5 * 10**9
    )
    return call(
        kernel(analysis_kernel), jax.ShapeDtypeStruct(arrived.shape, BF), (localized, deviation) + halo, 5 * 10**9
    )


def snake():
    columns, deep, cores = 4, 8, 2
    order = []
    for x in range(columns):
        for z in range(deep) if x % 2 == 0 else reversed(range(deep)):
            order += [(x * deep + z) * cores + core for core in range(cores)]
    return order


def on_device(ensemble, obs_cell, obs_count, obs_value, obs_rinv):
    order = snake()
    groups = lax.axis_size("mem")
    assert len(order) == groups
    local, cells = ensemble.shape

    def swapped(array, pairs):
        return lax.ppermute(array, "mem", pairs + [(target, source) for source, target in pairs])

    def swap_boundaries(across, partner):
        hops = [(order[i], order[(i + 1) % groups]) for i in range(1, groups, 2)]
        cores = [(order[i], order[i + 1]) for i in range(0, groups, 2)]
        return swapped(across, hops), swapped(partner, cores)

    def exchanged(array):
        return lax.all_to_all(array, "mem", split_axis=1, concat_axis=1, tiled=True, axis_index_groups=[order])

    arrived = exchanged(ensemble).reshape(local, groups, cells // groups).transpose(1, 0, 2)
    obs = packed(obs_cell[0], obs_count[0], obs_value[0], obs_rinv[0])
    obs = lax.ppermute(obs, "mem", list(enumerate(order)))
    outgoing = analyse(arrived, obs, swap_boundaries)
    return exchanged(outgoing.transpose(1, 0, 2).reshape(local, cells))


def solution(mesh):
    placed = (
        P("mem", "blk"),
        P("blk", "mem", None),
        P("blk", "mem"),
        P("blk", "mem", None),
        P("blk", "mem", None),
    )
    return jax.shard_map(
        on_device, mesh=mesh, in_specs=placed, out_specs=P("mem", "blk"), check_vma=False
    )
```

```python
import jax
import jax.numpy as jnp
from jax import lax
from jax.experimental import pallas as pl
from jax.experimental.pallas import tpu as pltpu
from jax.sharding import PartitionSpec as P

NS_ITERS = 4
localize = 0.5
inflation = 1.1

BF = jnp.bfloat16
F32 = jnp.float32
ROWS = 144


def split(a):
    high = a.astype(BF)
    return high, (a - high.astype(F32)).astype(BF)


def left_of(a):
    return jnp.concatenate(split(a), axis=1)


def right_of(a):
    pair = jnp.concatenate(split(a), axis=1)
    return jnp.concatenate([pair, pair], axis=0)


def fold(wide):
    half = wide.shape[1] // 2
    return wide[:, :half] + wide[:, half:]


def dot(a, b):
    return jnp.dot(a, b, preferred_element_type=F32)


def mm(left, right):
    return fold(dot(left, right))


def members_of(x_ref, b, width):
    piece = x_ref[:, :, b * width : (b + 1) * width]
    return piece.reshape(piece.shape[0] * piece.shape[1], width)


def sample(members, cells):
    position = lax.broadcasted_iota(jnp.int32, (members.shape[1], cells.shape[1]), 0)
    return dot(members, jnp.where(position == cells, 1.0, 0.0).astype(BF))


def weigh(sampled, count, obs_value, obs_rinv):
    size, slots = sampled.shape
    mean_at = jnp.sum(sampled, axis=0, keepdims=True) * (1.0 / size)
    slot = lax.broadcasted_iota(jnp.int32, (1, slots), 1)
    root = jnp.where(slot < count, jnp.sqrt(obs_rinv), 0.0)
    line = lax.broadcasted_iota(jnp.int32, (ROWS - size, slots), 0)
    lower = jnp.where(line == 0, root * (obs_value - mean_at), 0.0)
    return jnp.concatenate([((sampled - mean_at) * root).astype(BF), lower.astype(BF)], axis=0)


def rows_of(chosen, blocks, x_ref, cell_ref, count_ref, value_ref, rinv_ref):
    width = x_ref.shape[2] // blocks
    one = lambda b: slice(b, b + 1)
    sampled = [sample(members_of(x_ref, b, width), cell_ref[one(b)]) for b in chosen]
    return [
        weigh(s, count_ref[0:1, one(b)], value_ref[one(b)], rinv_ref[one(b)]) for b, s in zip(chosen, sampled)
    ]


def gram_of(rows):
    return lax.dot_general(rows, rows[:128], (((1,), (1,)), ((), ())), preferred_element_type=F32)


def eye_of(size):
    i = lax.broadcasted_iota(jnp.int32, (size, size), 0)
    j = lax.broadcasted_iota(jnp.int32, (size, size), 1)
    return jnp.where(i == j, 1.0, 0.0).astype(F32)


def transforms(localized, eye):
    size = eye.shape[0]
    systems = [g[:size] + (size - 1) / inflation * eye for g in localized]
    forcings = [g[size : size + 1] for g in localized]
    bounds = [
        jnp.max(jnp.sum(jnp.abs(a), axis=0, keepdims=True), axis=1, keepdims=True) for a in systems
    ]
    scales = [1.0 / b for b in bounds]
    y = [a * s for a, s in zip(systems, scales)]
    u = [1.5 * eye - 0.5 * a for a in y]
    z = u
    y = [mm(left_of(a), right_of(b)) for a, b in zip(y, u)]
    for iteration in range(NS_ITERS - 1):
        u = [1.5 * eye - 0.5 * mm(left_of(a), right_of(b)) for a, b in zip(z, y)]
        if iteration < NS_ITERS - 2:
            both = [
                mm(jnp.concatenate([left_of(a), left_of(c)], axis=0), right_of(b))
                for a, c, b in zip(y, z, u)
            ]
            y = [a[:size] for a in both]
            z = [a[size:] for a in both]
        else:
            z = [mm(left_of(a), right_of(b)) for a, b in zip(z, u)]
    out = []
    for a, f, s in zip(z, forcings, scales):
        inner = jnp.sum(a * f, axis=1, keepdims=True)
        weights = jnp.sum(a * inner, axis=0, keepdims=True) * s
        out.append(jnp.sqrt(s * (size - 1.0)) * a + weights - eye)
    return out


def apply_to(transform, members):
    size = transform.shape[0]
    pieces, rest = [], transform
    for _ in range(3):
        pieces.append(rest.astype(BF))
        rest = rest - pieces[-1].astype(F32)
    line = lax.broadcasted_iota(jnp.int32, (16, 3 * size), 0)
    lane = lax.broadcasted_iota(jnp.int32, (16, 3 * size), 1)
    ones = jnp.where(jnp.logical_and(line == 0, lane < size), 1.0, 0.0).astype(BF)
    left = jnp.concatenate([jnp.concatenate(pieces, axis=1), ones], axis=0)
    product = dot(left, jnp.concatenate([members] * 3, axis=0))
    average = product[size : size + 1] * (1.0 / size)
    return (product[:size] - jnp.sum(transform, axis=1, keepdims=True) * average).astype(BF)


def is_even():
    return lax.rem(lax.axis_index("mem"), 2) == 0


def boundary_kernel(blocks, x_ref, cell_ref, count_ref, value_ref, rinv_ref, across_ref, partner_ref):
    first, last = rows_of((0, blocks - 1), blocks, x_ref, cell_ref, count_ref, value_ref, rinv_ref)

    @pl.when(is_even())
    def _():
        across_ref[...] = first
        partner_ref[...] = last

    @pl.when(jnp.logical_not(is_even()))
    def _():
        across_ref[...] = last
        partner_ref[...] = first


def ordered(across_ref, partner_ref):
    across, partner = gram_of(across_ref[...]), gram_of(partner_ref[...])
    even = is_even()
    return jnp.where(even, across, partner), jnp.where(even, partner, across)


def finish(chosen, blocks, localized, x_ref, out_ref, offset):
    width = x_ref.shape[2] // blocks
    for b, transform in zip(chosen, transforms(localized, eye_of(128))):
        result = apply_to(transform, members_of(x_ref, b, width))
        place = slice((b + offset) * width, (b + offset + 1) * width)
        out_ref[:, :, place] = result.reshape(x_ref.shape[0], x_ref.shape[1], width)


def interior_kernel(
    blocks, x_ref, cell_ref, count_ref, value_ref, rinv_ref, across_ref, partner_ref, inner_ref, part_ref
):
    first, last = ordered(across_ref, partner_ref)
    chosen = range(1, blocks - 1)
    rows = rows_of(chosen, blocks, x_ref, cell_ref, count_ref, value_ref, rinv_ref)
    grams = [first] + [gram_of(r) for r in rows] + [last]
    part_ref[0] = grams[0] + localize * grams[1]
    part_ref[1] = grams[-1] + localize * grams[-2]
    localized = [grams[b] + localize * (grams[b - 1] + grams[b + 1]) for b in chosen]
    finish(chosen, blocks, localized, x_ref, inner_ref, -1)


def analysis_kernel(blocks, x_ref, part_ref, across_ref, partner_ref, inner_ref, out_ref):
    width = x_ref.shape[2] // blocks
    left, right = ordered(across_ref, partner_ref)
    localized = [part_ref[0] + localize * left, part_ref[1] + localize * right]
    out_ref[:, :, width : (blocks - 1) * width] = inner_ref[...]
    finish((0, blocks - 1), blocks, localized, x_ref, out_ref, 0)


VMEM = pl.BlockSpec(memory_space=pltpu.VMEM)


def call(kernel, out_shape, args, flops):
    outs = jax.tree.map(lambda _: VMEM, out_shape)
    moved = sum(a.size * a.dtype.itemsize for a in args)
    return pl.pallas_call(
        kernel,
        out_shape=out_shape,
        in_specs=[VMEM] * len(args),
        out_specs=outs,
        cost_estimate=pl.CostEstimate(flops=flops, bytes_accessed=moved, transcendentals=0),
        compiler_params=pltpu.CompilerParams(vmem_limit_bytes=40 * 2**20),
    )(*args)


def analyse(arrived, cells, counts, obs_value, obs_rinv, exchange):
    blocks, slots = cells.shape
    kernel = lambda body: (lambda *refs: body(blocks, *refs))
    rows = jax.ShapeDtypeStruct((ROWS, slots), BF)
    obs = (cells, counts, obs_value, obs_rinv)
    across, partner = call(kernel(boundary_kernel), (rows, rows), (arrived,) + obs, 2 * 10**8)
    halo = exchange(across, partner)
    inner = jax.ShapeDtypeStruct(arrived.shape[:2] + (arrived.shape[2] // blocks * (blocks - 2),), BF)
    part = jax.ShapeDtypeStruct((2, ROWS, 128), F32)
    inner, part = call(
        kernel(interior_kernel), (inner, part), (arrived,) + obs + (across, partner), 5 * 10**9
    )
    return call(
        kernel(analysis_kernel), jax.ShapeDtypeStruct(arrived.shape, BF), (arrived, part) + halo + (inner,), 2 * 10**9
    )


def swap_boundaries(across, partner):
    count = lax.axis_size("mem")
    hops = [(i, (i + 1) % count) for i in range(1, count, 2)]
    cores = [(i, i + 1) for i in range(0, count, 2)]
    both_ways = lambda pairs: pairs + [(target, source) for source, target in pairs]
    return lax.ppermute(across, "mem", both_ways(hops)), lax.ppermute(partner, "mem", both_ways(cores))


def on_device(ensemble, obs_cell, obs_count, obs_value, obs_rinv):
    groups = lax.axis_size("mem")
    local, cells = ensemble.shape
    arrived = lax.all_to_all(ensemble, "mem", split_axis=1, concat_axis=1, tiled=True)
    arrived = arrived.reshape(local, groups, cells // groups).transpose(1, 0, 2)
    outgoing = analyse(arrived, obs_cell[0], obs_count, obs_value[0], obs_rinv[0], swap_boundaries)
    outgoing = outgoing.transpose(1, 0, 2).reshape(local, cells)
    return lax.all_to_all(outgoing, "mem", split_axis=1, concat_axis=1, tiled=True)


def solution(mesh):
    placed = (
        P("mem", "blk"),
        P("blk", "mem", None),
        P("blk", "mem"),
        P("blk", "mem", None),
        P("blk", "mem", None),
    )
    return jax.shard_map(
        on_device, mesh=mesh, in_specs=placed, out_specs=P("mem", "blk"), check_vma=False
    )
```

```python
import jax
import jax.numpy as jnp
from jax import lax
from jax.experimental import pallas as pl
from jax.experimental.pallas import tpu as pltpu
from jax.sharding import PartitionSpec as P

NS_ITERS = 4
localize = 0.5
inflation = 1.1

BF = jnp.bfloat16
F32 = jnp.float32
ROWS = 144


def split(a):
    high = a.astype(BF)
    return high, (a - high.astype(F32)).astype(BF)


def left_of(a):
    return jnp.concatenate(split(a), axis=1)


def right_of(a):
    pair = jnp.concatenate(split(a), axis=1)
    return jnp.concatenate([pair, pair], axis=0)


def fold(wide):
    half = wide.shape[1] // 2
    return wide[:, :half] + wide[:, half:]


def dot(a, b):
    return jnp.dot(a, b, preferred_element_type=F32)


def mm(left, right):
    return fold(dot(left, right))


def members_of(x_ref, b, width):
    piece = x_ref[:, :, b * width : (b + 1) * width]
    return piece.reshape(piece.shape[0] * piece.shape[1], width)


def sample(members, cells):
    position = lax.broadcasted_iota(jnp.int32, (members.shape[1], cells.shape[1]), 0)
    return dot(members, jnp.where(position == cells, 1.0, 0.0).astype(BF))


def weigh(sampled, obs_value, root):
    size, slots = sampled.shape
    mean_at = jnp.sum(sampled, axis=0, keepdims=True) * (1.0 / size)
    line = lax.broadcasted_iota(jnp.int32, (ROWS - size, slots), 0)
    lower = jnp.where(line == 0, root * (obs_value - mean_at), 0.0)
    return jnp.concatenate([((sampled - mean_at) * root).astype(BF), lower.astype(BF)], axis=0)


def rows_of(chosen, blocks, x_ref, obs_ref):
    width = x_ref.shape[2] // blocks
    of_kind = lambda kind, b: obs_ref[kind * blocks + b : kind * blocks + b + 1]
    sampled = [sample(members_of(x_ref, b, width), of_kind(0, b).astype(jnp.int32)) for b in chosen]
    return [weigh(s, of_kind(1, b), of_kind(2, b)) for b, s in zip(chosen, sampled)]


def gram_of(rows):
    return lax.dot_general(rows, rows[:128], (((1,), (1,)), ((), ())), preferred_element_type=F32)


def eye_of(size):
    i = lax.broadcasted_iota(jnp.int32, (size, size), 0)
    j = lax.broadcasted_iota(jnp.int32, (size, size), 1)
    return jnp.where(i == j, 1.0, 0.0).astype(F32)


def transforms(localized, eye):
    size = eye.shape[0]
    systems = [g[:size] + (size - 1) / inflation * eye for g in localized]
    forcings = [g[size : size + 1] for g in localized]
    bounds = [
        jnp.max(jnp.sum(jnp.abs(a), axis=0, keepdims=True), axis=1, keepdims=True) for a in systems
    ]
    scales = [1.0 / b for b in bounds]
    y = [a * s for a, s in zip(systems, scales)]
    u = [1.5 * eye - 0.5 * a for a in y]
    z = u
    y = [mm(left_of(a), right_of(b)) for a, b in zip(y, u)]
    for iteration in range(NS_ITERS - 1):
        u = [1.5 * eye - 0.5 * mm(left_of(a), right_of(b)) for a, b in zip(z, y)]
        if iteration < NS_ITERS - 2:
            both = [
                mm(jnp.concatenate([left_of(a), left_of(c)], axis=0), right_of(b))
                for a, c, b in zip(y, z, u)
            ]
            y = [a[:size] for a in both]
            z = [a[size:] for a in both]
        else:
            z = [mm(left_of(a), right_of(b)) for a, b in zip(z, u)]
    out = []
    for a, f, s in zip(z, forcings, scales):
        inner = jnp.sum(a * f, axis=1, keepdims=True)
        weights = jnp.sum(a * inner, axis=0, keepdims=True) * s
        out.append(jnp.sqrt(s * (size - 1.0)) * a + weights - eye)
    return out


def apply_to(transform, members):
    size = transform.shape[0]
    pieces, rest = [], transform
    for _ in range(3):
        pieces.append(rest.astype(BF))
        rest = rest - pieces[-1].astype(F32)
    line = lax.broadcasted_iota(jnp.int32, (16, 3 * size), 0)
    lane = lax.broadcasted_iota(jnp.int32, (16, 3 * size), 1)
    ones = jnp.where(jnp.logical_and(line == 0, lane < size), 1.0, 0.0).astype(BF)
    left = jnp.concatenate([jnp.concatenate(pieces, axis=1), ones], axis=0)
    product = dot(left, jnp.concatenate([members] * 3, axis=0))
    average = product[size : size + 1] * (1.0 / size)
    return (product[:size] - jnp.sum(transform, axis=1, keepdims=True) * average).astype(BF)


def is_even():
    return lax.rem(lax.axis_index("mem"), 2) == 0


def boundary_kernel(blocks, x_ref, obs_ref, across_ref, partner_ref):
    first, last = rows_of((0, blocks - 1), blocks, x_ref, obs_ref)

    @pl.when(is_even())
    def _():
        across_ref[...] = first
        partner_ref[...] = last

    @pl.when(jnp.logical_not(is_even()))
    def _():
        across_ref[...] = last
        partner_ref[...] = first


def ordered(across_ref, partner_ref):
    across, partner = gram_of(across_ref[...]), gram_of(partner_ref[...])
    even = is_even()
    return jnp.where(even, across, partner), jnp.where(even, partner, across)


def finish(chosen, blocks, localized, x_ref, out_ref, offset):
    width = x_ref.shape[2] // blocks
    for b, transform in zip(chosen, transforms(localized, eye_of(128))):
        result = apply_to(transform, members_of(x_ref, b, width))
        place = slice((b + offset) * width, (b + offset + 1) * width)
        out_ref[:, :, place] = result.reshape(x_ref.shape[0], x_ref.shape[1], width)


def interior_kernel(
    blocks, x_ref, obs_ref, across_ref, partner_ref, inner_ref, part_ref
):
    first, last = ordered(across_ref, partner_ref)
    chosen = range(1, blocks - 1)
    rows = rows_of(chosen, blocks, x_ref, obs_ref)
    grams = [first] + [gram_of(r) for r in rows] + [last]
    part_ref[0] = grams[0] + localize * grams[1]
    part_ref[1] = grams[-1] + localize * grams[-2]
    localized = [grams[b] + localize * (grams[b - 1] + grams[b + 1]) for b in chosen]
    finish(chosen, blocks, localized, x_ref, inner_ref, -1)


def analysis_kernel(blocks, x_ref, part_ref, across_ref, partner_ref, inner_ref, out_ref):
    width = x_ref.shape[2] // blocks
    left, right = ordered(across_ref, partner_ref)
    localized = [part_ref[0] + localize * left, part_ref[1] + localize * right]
    out_ref[:, :, width : (blocks - 1) * width] = inner_ref[...]
    finish((0, blocks - 1), blocks, localized, x_ref, out_ref, 0)


VMEM = pl.BlockSpec(memory_space=pltpu.VMEM)


def call(kernel, out_shape, args, flops):
    outs = jax.tree.map(lambda _: VMEM, out_shape)
    moved = sum(a.size * a.dtype.itemsize for a in args)
    return pl.pallas_call(
        kernel,
        out_shape=out_shape,
        in_specs=[VMEM] * len(args),
        out_specs=outs,
        cost_estimate=pl.CostEstimate(flops=flops, bytes_accessed=moved, transcendentals=0),
        compiler_params=pltpu.CompilerParams(vmem_limit_bytes=40 * 2**20),
    )(*args)


def packed(obs_cell, obs_count, obs_value, obs_rinv):
    slot = lax.broadcasted_iota(jnp.int32, obs_cell.shape, 1)
    root = jnp.where(slot < obs_count[:, None], jnp.sqrt(obs_rinv), 0.0)
    return jnp.concatenate([obs_cell.astype(F32), obs_value, root], axis=0)


def analyse(arrived, obs, exchange):
    blocks, slots = obs.shape[0] // 3, obs.shape[1]
    kernel = lambda body: (lambda *refs: body(blocks, *refs))
    rows = jax.ShapeDtypeStruct((ROWS, slots), BF)
    across, partner = call(kernel(boundary_kernel), (rows, rows), (arrived, obs), 2 * 10**8)
    halo = exchange(across, partner)
    inner = jax.ShapeDtypeStruct(arrived.shape[:2] + (arrived.shape[2] // blocks * (blocks - 2),), BF)
    part = jax.ShapeDtypeStruct((2, ROWS, 128), F32)
    inner, part = call(
        kernel(interior_kernel), (inner, part), (arrived, obs, across, partner), 5 * 10**9
    )
    return call(
        kernel(analysis_kernel), jax.ShapeDtypeStruct(arrived.shape, BF), (arrived, part) + halo + (inner,), 2 * 10**9
    )


def swap_boundaries(across, partner):
    count = lax.axis_size("mem")
    hops = [(i, (i + 1) % count) for i in range(1, count, 2)]
    cores = [(i, i + 1) for i in range(0, count, 2)]
    both_ways = lambda pairs: pairs + [(target, source) for source, target in pairs]
    return lax.ppermute(across, "mem", both_ways(hops)), lax.ppermute(partner, "mem", both_ways(cores))


def on_device(ensemble, obs_cell, obs_count, obs_value, obs_rinv):
    groups = lax.axis_size("mem")
    local, cells = ensemble.shape
    arrived = lax.all_to_all(ensemble, "mem", split_axis=1, concat_axis=1, tiled=True)
    arrived = arrived.reshape(local, groups, cells // groups).transpose(1, 0, 2)
    obs = packed(obs_cell[0], obs_count[0], obs_value[0], obs_rinv[0])
    outgoing = analyse(arrived, obs, swap_boundaries)
    outgoing = outgoing.transpose(1, 0, 2).reshape(local, cells)
    return lax.all_to_all(outgoing, "mem", split_axis=1, concat_axis=1, tiled=True)


def solution(mesh):
    placed = (
        P("mem", "blk"),
        P("blk", "mem", None),
        P("blk", "mem"),
        P("blk", "mem", None),
        P("blk", "mem", None),
    )
    return jax.shard_map(
        on_device, mesh=mesh, in_specs=placed, out_specs=P("mem", "blk"), check_vma=False
    )
```

```python
import jax
import jax.numpy as jnp
from jax import lax
from jax.experimental import pallas as pl
from jax.experimental.pallas import tpu as pltpu
from jax.sharding import PartitionSpec as P

NS_ITERS = 4
localize = 0.5
inflation = 1.1

BF = jnp.bfloat16
F32 = jnp.float32
ROWS = 144


def split(a):
    high = a.astype(BF)
    return high, (a - high.astype(F32)).astype(BF)


def left_of(a):
    high, low = split(a)
    return jnp.concatenate([high, low, high], axis=1)


def right_of(a):
    high, low = split(a)
    return jnp.concatenate([high, high, low], axis=0)


def dot(a, b):
    return jnp.dot(a, b, preferred_element_type=F32)


def members_of(x_ref, b, width):
    piece = x_ref[:, :, b * width : (b + 1) * width]
    return piece.reshape(piece.shape[0] * piece.shape[1], width)


def sample(members, cells):
    position = lax.broadcasted_iota(jnp.int32, (members.shape[1], cells.shape[1]), 0)
    return dot(members, jnp.where(position == cells, 1.0, 0.0).astype(BF))


def weigh(sampled, obs_value, root):
    size, slots = sampled.shape
    mean_at = jnp.sum(sampled, axis=0, keepdims=True) * (1.0 / size)
    line = lax.broadcasted_iota(jnp.int32, (ROWS - size, slots), 0)
    lower = jnp.where(line == 0, root * (obs_value - mean_at), 0.0)
    return jnp.concatenate([((sampled - mean_at) * root).astype(BF), lower.astype(BF)], axis=0)


def rows_of(chosen, blocks, x_ref, obs_ref):
    width = x_ref.shape[2] // blocks
    of_kind = lambda kind, b: obs_ref[kind * blocks + b : kind * blocks + b + 1]
    sampled = [sample(members_of(x_ref, b, width), of_kind(0, b).astype(jnp.int32)) for b in chosen]
    return [weigh(s, of_kind(1, b), of_kind(2, b)) for b, s in zip(chosen, sampled)]


def gram_of(rows):
    return lax.dot_general(rows, rows[:128], (((1,), (1,)), ((), ())), preferred_element_type=F32)


def eye_of(size):
    i = lax.broadcasted_iota(jnp.int32, (size, size), 0)
    j = lax.broadcasted_iota(jnp.int32, (size, size), 1)
    return jnp.where(i == j, 1.0, 0.0).astype(F32)


def transforms(localized, eye):
    size = eye.shape[0]
    systems = [g[:size] + (size - 1) / inflation * eye for g in localized]
    forcings = [g[size : size + 1] for g in localized]
    bounds = [
        jnp.max(jnp.sum(jnp.abs(a), axis=0, keepdims=True), axis=1, keepdims=True) for a in systems
    ]
    scales = [1.0 / b for b in bounds]
    squares = [dot(left_of(a), right_of(a)) for a in systems]
    y = [s * (1.5 * a - (0.5 * s) * q) for a, q, s in zip(systems, squares, scales)]
    z = [1.5 * eye - (0.5 * s) * a for a, s in zip(systems, scales)]
    for iteration in range(NS_ITERS - 1):
        u = [1.5 * eye - 0.5 * dot(left_of(a), right_of(b)) for a, b in zip(z, y)]
        if iteration < NS_ITERS - 2:
            both = [
                dot(jnp.concatenate([left_of(a), left_of(c)], axis=0), right_of(b))
                for a, c, b in zip(y, z, u)
            ]
            y = [a[:size] for a in both]
            z = [a[size:] for a in both]
        else:
            z = [dot(left_of(a), right_of(b)) for a, b in zip(z, u)]
    out = []
    for a, f, s in zip(z, forcings, scales):
        inner = jnp.sum(a * f, axis=1, keepdims=True)
        weights = jnp.sum(a * inner, axis=0, keepdims=True) * s
        out.append(jnp.sqrt(s * (size - 1.0)) * a + weights - eye)
    return out


def apply_to(transform, members):
    size = transform.shape[0]
    pieces, rest = [], transform
    for _ in range(3):
        pieces.append(rest.astype(BF))
        rest = rest - pieces[-1].astype(F32)
    line = lax.broadcasted_iota(jnp.int32, (16, 3 * size), 0)
    lane = lax.broadcasted_iota(jnp.int32, (16, 3 * size), 1)
    ones = jnp.where(jnp.logical_and(line == 0, lane < size), 1.0, 0.0).astype(BF)
    left = jnp.concatenate([jnp.concatenate(pieces, axis=1), ones], axis=0)
    product = dot(left, jnp.concatenate([members] * 3, axis=0))
    average = product[size : size + 1] * (1.0 / size)
    return (product[:size] - jnp.sum(transform, axis=1, keepdims=True) * average).astype(BF)


def is_even():
    return lax.rem(lax.axis_index("mem"), 2) == 0


def boundary_kernel(blocks, x_ref, obs_ref, across_ref, partner_ref):
    first, last = rows_of((0, blocks - 1), blocks, x_ref, obs_ref)

    @pl.when(is_even())
    def _():
        across_ref[...] = first
        partner_ref[...] = last

    @pl.when(jnp.logical_not(is_even()))
    def _():
        across_ref[...] = last
        partner_ref[...] = first


def ordered(across_ref, partner_ref):
    across, partner = gram_of(across_ref[...]), gram_of(partner_ref[...])
    even = is_even()
    return jnp.where(even, across, partner), jnp.where(even, partner, across)


def finish(places, localized, members, out_ref):
    for place, transform, load in zip(places, transforms(localized, eye_of(128)), members):
        result = apply_to(transform, load())
        width = result.shape[1]
        out_ref[:, :, place * width : (place + 1) * width] = result.reshape(out_ref.shape[:2] + (width,))


def interior_kernel(
    blocks, x_ref, obs_ref, across_ref, partner_ref, inner_ref, part_ref, edge_ref
):
    first, last = ordered(across_ref, partner_ref)
    chosen = range(1, blocks - 1)
    rows = rows_of(chosen, blocks, x_ref, obs_ref)
    grams = [first] + [gram_of(r) for r in rows] + [last]
    part_ref[0] = grams[0] + localize * grams[1]
    part_ref[1] = grams[-1] + localize * grams[-2]
    localized = [grams[b] + localize * (grams[b - 1] + grams[b + 1]) for b in chosen]
    width = x_ref.shape[2] // blocks
    edge_ref[0] = members_of(x_ref, 0, width)
    edge_ref[1] = members_of(x_ref, blocks - 1, width)
    members = [lambda b=b: members_of(x_ref, b, width) for b in chosen]
    finish([b - 1 for b in chosen], localized, members, inner_ref)


def analysis_kernel(blocks, edge_ref, part_ref, across_ref, partner_ref, inner_ref, out_ref):
    width = edge_ref.shape[2]
    left, right = ordered(across_ref, partner_ref)
    localized = [part_ref[0] + localize * left, part_ref[1] + localize * right]
    out_ref[:, :, width : (blocks - 1) * width] = inner_ref[...]
    finish((0, blocks - 1), localized, [lambda: edge_ref[0], lambda: edge_ref[1]], out_ref)


VMEM = pl.BlockSpec(memory_space=pltpu.VMEM)


def call(kernel, out_shape, args, flops):
    outs = jax.tree.map(lambda _: VMEM, out_shape)
    moved = sum(a.size * a.dtype.itemsize for a in args)
    return pl.pallas_call(
        kernel,
        out_shape=out_shape,
        in_specs=[VMEM] * len(args),
        out_specs=outs,
        cost_estimate=pl.CostEstimate(flops=flops, bytes_accessed=moved, transcendentals=0),
        compiler_params=pltpu.CompilerParams(vmem_limit_bytes=40 * 2**20),
    )(*args)


def packed(obs_cell, obs_count, obs_value, obs_rinv):
    slot = lax.broadcasted_iota(jnp.int32, obs_cell.shape, 1)
    root = jnp.where(slot < obs_count[:, None], jnp.sqrt(obs_rinv), 0.0)
    return jnp.concatenate([obs_cell.astype(F32), obs_value, root], axis=0)


def analyse(arrived, obs, exchange):
    blocks, slots = obs.shape[0] // 3, obs.shape[1]
    kernel = lambda body: (lambda *refs: body(blocks, *refs))
    rows = jax.ShapeDtypeStruct((ROWS, slots), BF)
    across, partner = call(kernel(boundary_kernel), (rows, rows), (arrived, obs), 2 * 10**8)
    halo = exchange(across, partner)
    inner = jax.ShapeDtypeStruct(arrived.shape[:2] + (arrived.shape[2] // blocks * (blocks - 2),), BF)
    part = jax.ShapeDtypeStruct((2, ROWS, 128), F32)
    edge = jax.ShapeDtypeStruct((2, 128, arrived.shape[2] // blocks), BF)
    inner, part, edge = call(
        kernel(interior_kernel), (inner, part, edge), (arrived, obs, across, partner), 5 * 10**9
    )
    return call(
        kernel(analysis_kernel), jax.ShapeDtypeStruct(arrived.shape, BF), (edge, part) + halo + (inner,), 2 * 10**9
    )


def swap_boundaries(across, partner):
    count = lax.axis_size("mem")
    hops = [(i, (i + 1) % count) for i in range(1, count, 2)]
    cores = [(i, i + 1) for i in range(0, count, 2)]
    both_ways = lambda pairs: pairs + [(target, source) for source, target in pairs]
    return lax.ppermute(across, "mem", both_ways(hops)), lax.ppermute(partner, "mem", both_ways(cores))


def on_device(ensemble, obs_cell, obs_count, obs_value, obs_rinv):
    groups = lax.axis_size("mem")
    local, cells = ensemble.shape
    arrived = lax.all_to_all(ensemble, "mem", split_axis=1, concat_axis=1, tiled=True)
    arrived = arrived.reshape(local, groups, cells // groups).transpose(1, 0, 2)
    obs = packed(obs_cell[0], obs_count[0], obs_value[0], obs_rinv[0])
    outgoing = analyse(arrived, obs, swap_boundaries)
    outgoing = outgoing.transpose(1, 0, 2).reshape(local, cells)
    return lax.all_to_all(outgoing, "mem", split_axis=1, concat_axis=1, tiled=True)


def solution(mesh):
    placed = (
        P("mem", "blk"),
        P("blk", "mem", None),
        P("blk", "mem"),
        P("blk", "mem", None),
        P("blk", "mem", None),
    )
    return jax.shard_map(
        on_device, mesh=mesh, in_specs=placed, out_specs=P("mem", "blk"), check_vma=False
    )
```

```python
import jax
import jax.numpy as jnp
from jax import lax
from jax.experimental import pallas as pl
from jax.experimental.pallas import tpu as pltpu
from jax.sharding import PartitionSpec as P

NS_ITERS = 4
localize = 0.5
inflation = 1.1

BF = jnp.bfloat16
F32 = jnp.float32
ROWS = 144


def split(a):
    high = a.astype(BF)
    return high, (a - high.astype(F32)).astype(BF)


def left_of(a):
    high, low = split(a)
    return jnp.concatenate([high, low, high], axis=1)


def right_of(a):
    high, low = split(a)
    return jnp.concatenate([high, high, low], axis=0)


def dot(a, b):
    return jnp.dot(a, b, preferred_element_type=F32)


def members_of(x_ref, b, width):
    piece = x_ref[:, :, b * width : (b + 1) * width]
    return piece.reshape(piece.shape[0] * piece.shape[1], width)


def sample(members, cells):
    position = lax.broadcasted_iota(jnp.int32, (members.shape[1], cells.shape[1]), 0)
    return dot(members, jnp.where(position == cells, 1.0, 0.0).astype(BF))


def weigh(sampled, obs_value, root):
    size, slots = sampled.shape
    mean_at = jnp.sum(sampled, axis=0, keepdims=True) * (1.0 / size)
    line = lax.broadcasted_iota(jnp.int32, (ROWS - size, slots), 0)
    lower = jnp.where(line == 0, root * (obs_value - mean_at), 0.0)
    return jnp.concatenate([((sampled - mean_at) * root).astype(BF), lower.astype(BF)], axis=0)


def rows_of(chosen, blocks, x_ref, obs_ref):
    width = x_ref.shape[2] // blocks
    of_kind = lambda kind, b: obs_ref[kind * blocks + b : kind * blocks + b + 1]
    sampled = [sample(members_of(x_ref, b, width), of_kind(0, b).astype(jnp.int32)) for b in chosen]
    return [weigh(s, of_kind(1, b), of_kind(2, b)) for b, s in zip(chosen, sampled)]


def gram_of(rows):
    return lax.dot_general(rows, rows[:128], (((1,), (1,)), ((), ())), preferred_element_type=F32)


def eye_of(size):
    i = lax.broadcasted_iota(jnp.int32, (size, size), 0)
    j = lax.broadcasted_iota(jnp.int32, (size, size), 1)
    return jnp.where(i == j, 1.0, 0.0).astype(F32)


def transforms(localized, eye):
    size = eye.shape[0]
    systems = [g[:size] + (size - 1) / inflation * eye for g in localized]
    forcings = [g[size : size + 1] for g in localized]
    bounds = [
        jnp.max(jnp.sum(jnp.abs(a), axis=0, keepdims=True), axis=1, keepdims=True) for a in systems
    ]
    scales = [1.0 / b for b in bounds]
    squares = [dot(left_of(a), right_of(a)) for a in systems]
    y = [s * (1.5 * a - (0.5 * s) * q) for a, q, s in zip(systems, squares, scales)]
    z = [1.5 * eye - (0.5 * s) * a for a, s in zip(systems, scales)]
    for iteration in range(NS_ITERS - 1):
        u = [1.5 * eye - 0.5 * dot(left_of(a), right_of(b)) for a, b in zip(z, y)]
        if iteration < NS_ITERS - 2:
            both = [
                dot(jnp.concatenate([left_of(a), left_of(c)], axis=0), right_of(b))
                for a, c, b in zip(y, z, u)
            ]
            y = [a[:size] for a in both]
            z = [a[size:] for a in both]
        else:
            z = [dot(left_of(a), right_of(b)) for a, b in zip(z, u)]
    out = []
    for a, f, s in zip(z, forcings, scales):
        inner = jnp.sum(a * f, axis=1, keepdims=True)
        weights = jnp.sum(a * inner, axis=0, keepdims=True) * s
        out.append(jnp.sqrt(s * (size - 1.0)) * a + weights - eye)
    return out


def apply_to(transform, members):
    size = transform.shape[0]
    high, low = split(transform)
    held = high.astype(F32) + low.astype(F32)
    line = lax.broadcasted_iota(jnp.int32, (16, 2 * size), 0)
    lane = lax.broadcasted_iota(jnp.int32, (16, 2 * size), 1)
    ones = jnp.where(jnp.logical_and(line == 0, lane < size), 1.0, 0.0).astype(BF)
    left = jnp.concatenate([jnp.concatenate([high, low], axis=1), ones], axis=0)
    product = dot(left, jnp.concatenate([members] * 2, axis=0))
    average = product[size : size + 1] * (1.0 / size)
    return (product[:size] - jnp.sum(held, axis=1, keepdims=True) * average).astype(BF)


def is_even():
    return lax.rem(lax.axis_index("mem"), 2) == 0


def boundary_kernel(blocks, x_ref, obs_ref, across_ref, partner_ref):
    first, last = rows_of((0, blocks - 1), blocks, x_ref, obs_ref)

    @pl.when(is_even())
    def _():
        across_ref[...] = first
        partner_ref[...] = last

    @pl.when(jnp.logical_not(is_even()))
    def _():
        across_ref[...] = last
        partner_ref[...] = first


def ordered(across_ref, partner_ref):
    across, partner = gram_of(across_ref[...]), gram_of(partner_ref[...])
    even = is_even()
    return jnp.where(even, across, partner), jnp.where(even, partner, across)


def finish(places, localized, members, out_ref):
    for place, transform, load in zip(places, transforms(localized, eye_of(128)), members):
        result = apply_to(transform, load())
        width = result.shape[1]
        out_ref[:, :, place * width : (place + 1) * width] = result.reshape(out_ref.shape[:2] + (width,))


def interior_kernel(
    blocks, x_ref, obs_ref, across_ref, partner_ref, inner_ref, part_ref, edge_ref
):
    first, last = ordered(across_ref, partner_ref)
    chosen = range(1, blocks - 1)
    rows = rows_of(chosen, blocks, x_ref, obs_ref)
    grams = [first] + [gram_of(r) for r in rows] + [last]
    part_ref[0] = grams[0] + localize * grams[1]
    part_ref[1] = grams[-1] + localize * grams[-2]
    localized = [grams[b] + localize * (grams[b - 1] + grams[b + 1]) for b in chosen]
    width = x_ref.shape[2] // blocks
    edge_ref[0] = members_of(x_ref, 0, width)
    edge_ref[1] = members_of(x_ref, blocks - 1, width)
    members = [lambda b=b: members_of(x_ref, b, width) for b in chosen]
    finish([b - 1 for b in chosen], localized, members, inner_ref)


def analysis_kernel(blocks, edge_ref, part_ref, across_ref, partner_ref, inner_ref, out_ref):
    width = edge_ref.shape[2]
    left, right = ordered(across_ref, partner_ref)
    localized = [part_ref[0] + localize * left, part_ref[1] + localize * right]
    out_ref[:, :, width : (blocks - 1) * width] = inner_ref[...]
    finish((0, blocks - 1), localized, [lambda: edge_ref[0], lambda: edge_ref[1]], out_ref)


VMEM = pl.BlockSpec(memory_space=pltpu.VMEM)


def call(kernel, out_shape, args, flops):
    outs = jax.tree.map(lambda _: VMEM, out_shape)
    moved = sum(a.size * a.dtype.itemsize for a in args)
    return pl.pallas_call(
        kernel,
        out_shape=out_shape,
        in_specs=[VMEM] * len(args),
        out_specs=outs,
        cost_estimate=pl.CostEstimate(flops=flops, bytes_accessed=moved, transcendentals=0),
        compiler_params=pltpu.CompilerParams(vmem_limit_bytes=40 * 2**20),
    )(*args)


def packed(obs_cell, obs_count, obs_value, obs_rinv):
    slot = lax.broadcasted_iota(jnp.int32, obs_cell.shape, 1)
    root = jnp.where(slot < obs_count[:, None], jnp.sqrt(obs_rinv), 0.0)
    return jnp.concatenate([obs_cell.astype(F32), obs_value, root], axis=0)


def analyse(arrived, obs, exchange):
    blocks, slots = obs.shape[0] // 3, obs.shape[1]
    kernel = lambda body: (lambda *refs: body(blocks, *refs))
    rows = jax.ShapeDtypeStruct((ROWS, slots), BF)
    across, partner = call(kernel(boundary_kernel), (rows, rows), (arrived, obs), 2 * 10**8)
    halo = exchange(across, partner)
    inner = jax.ShapeDtypeStruct(arrived.shape[:2] + (arrived.shape[2] // blocks * (blocks - 2),), BF)
    part = jax.ShapeDtypeStruct((2, ROWS, 128), F32)
    edge = jax.ShapeDtypeStruct((2, 128, arrived.shape[2] // blocks), BF)
    inner, part, edge = call(
        kernel(interior_kernel), (inner, part, edge), (arrived, obs, across, partner), 5 * 10**9
    )
    return call(
        kernel(analysis_kernel), jax.ShapeDtypeStruct(arrived.shape, BF), (edge, part) + halo + (inner,), 2 * 10**9
    )


def swap_boundaries(across, partner):
    count = lax.axis_size("mem")
    hops = [(i, (i + 1) % count) for i in range(1, count, 2)]
    cores = [(i, i + 1) for i in range(0, count, 2)]
    both_ways = lambda pairs: pairs + [(target, source) for source, target in pairs]
    return lax.ppermute(across, "mem", both_ways(hops)), lax.ppermute(partner, "mem", both_ways(cores))


def on_device(ensemble, obs_cell, obs_count, obs_value, obs_rinv):
    groups = lax.axis_size("mem")
    local, cells = ensemble.shape
    arrived = lax.all_to_all(ensemble, "mem", split_axis=1, concat_axis=1, tiled=True)
    arrived = arrived.reshape(local, groups, cells // groups).transpose(1, 0, 2)
    obs = packed(obs_cell[0], obs_count[0], obs_value[0], obs_rinv[0])
    outgoing = analyse(arrived, obs, swap_boundaries)
    outgoing = outgoing.transpose(1, 0, 2).reshape(local, cells)
    return lax.all_to_all(outgoing, "mem", split_axis=1, concat_axis=1, tiled=True)


def solution(mesh):
    placed = (
        P("mem", "blk"),
        P("blk", "mem", None),
        P("blk", "mem"),
        P("blk", "mem", None),
        P("blk", "mem", None),
    )
    return jax.shard_map(
        on_device, mesh=mesh, in_specs=placed, out_specs=P("mem", "blk"), check_vma=False
    )
```

```python
import jax
import jax.numpy as jnp
from jax import lax
from jax.experimental import pallas as pl
from jax.experimental.pallas import tpu as pltpu
from jax.sharding import PartitionSpec as P

NS_ITERS = 4
localize = 0.5
inflation = 1.1

BF = jnp.bfloat16
F32 = jnp.float32
ROWS = 144


def split(a):
    high = a.astype(BF)
    return high, (a - high.astype(F32)).astype(BF)


def left_of(a):
    high, low = split(a)
    return jnp.concatenate([high, low, high], axis=1)


def right_of(a):
    high, low = split(a)
    return jnp.concatenate([high, high, low], axis=0)


def dot(a, b):
    return jnp.dot(a, b, preferred_element_type=F32)


def members_of(x_ref, b, width):
    piece = x_ref[:, :, b * width : (b + 1) * width]
    return piece.reshape(piece.shape[0] * piece.shape[1], width)


def sample(members, cells):
    position = lax.broadcasted_iota(jnp.int32, (members.shape[1], cells.shape[1]), 0)
    return dot(members, jnp.where(position == cells, 1.0, 0.0).astype(BF))


def weigh(sampled, obs_value, root):
    size, slots = sampled.shape
    mean_at = jnp.sum(sampled, axis=0, keepdims=True) * (1.0 / size)
    line = lax.broadcasted_iota(jnp.int32, (ROWS - size, slots), 0)
    lower = jnp.where(line == 0, root * (obs_value - mean_at), 0.0)
    return jnp.concatenate([((sampled - mean_at) * root).astype(BF), lower.astype(BF)], axis=0)


def rows_of(chosen, blocks, x_ref, obs_ref):
    width = x_ref.shape[2] // blocks
    of_kind = lambda kind, b: obs_ref[kind * blocks + b : kind * blocks + b + 1]
    sampled = [sample(members_of(x_ref, b, width), of_kind(0, b).astype(jnp.int32)) for b in chosen]
    return [weigh(s, of_kind(1, b), of_kind(2, b)) for b, s in zip(chosen, sampled)]


def gram_of(rows):
    return lax.dot_general(rows, rows[:128], (((1,), (1,)), ((), ())), preferred_element_type=F32)


def eye_of(size):
    i = lax.broadcasted_iota(jnp.int32, (size, size), 0)
    j = lax.broadcasted_iota(jnp.int32, (size, size), 1)
    return jnp.where(i == j, 1.0, 0.0).astype(F32)


def transforms(localized, eye):
    size = eye.shape[0]
    systems = [g[:size] + (size - 1) / inflation * eye for g in localized]
    forcings = [g[size : size + 1] for g in localized]
    bounds = [
        jnp.max(jnp.sum(jnp.abs(a), axis=0, keepdims=True), axis=1, keepdims=True) for a in systems
    ]
    scales = [1.0 / b for b in bounds]
    squares = [dot(left_of(a), right_of(a)) for a in systems]
    y = [s * (1.5 * a - (0.5 * s) * q) for a, q, s in zip(systems, squares, scales)]
    z = [1.5 * eye - (0.5 * s) * a for a, s in zip(systems, scales)]
    for iteration in range(NS_ITERS - 1):
        u = [1.5 * eye - 0.5 * dot(left_of(a), right_of(b)) for a, b in zip(z, y)]
        if iteration < NS_ITERS - 2:
            both = [
                dot(jnp.concatenate([left_of(a), left_of(c)], axis=0), right_of(b))
                for a, c, b in zip(y, z, u)
            ]
            y = [a[:size] for a in both]
            z = [a[size:] for a in both]
        else:
            columns = [jnp.sum(eye * f, axis=1, keepdims=True) for f in forcings]
            early = [jnp.sum(a * c, axis=0, keepdims=True) for a, c in zip(z, columns)]
            inner = [jnp.sum(b * e, axis=1, keepdims=True) for b, e in zip(u, early)]
            z = [dot(left_of(a), right_of(b)) for a, b in zip(z, u)]
    out = []
    for a, i, s in zip(z, inner, scales):
        weights = jnp.sum(a * i, axis=0, keepdims=True) * s
        out.append(jnp.sqrt(s * (size - 1.0)) * a + weights - eye)
    return out


def apply_to(transform, members):
    size = transform.shape[0]
    high, low = split(transform)
    held = high.astype(F32) + low.astype(F32)
    line = lax.broadcasted_iota(jnp.int32, (16, 2 * size), 0)
    lane = lax.broadcasted_iota(jnp.int32, (16, 2 * size), 1)
    ones = jnp.where(jnp.logical_and(line == 0, lane < size), 1.0, 0.0).astype(BF)
    left = jnp.concatenate([jnp.concatenate([high, low], axis=1), ones], axis=0)
    product = dot(left, jnp.concatenate([members] * 2, axis=0))
    average = product[size : size + 1] * (1.0 / size)
    return (product[:size] - jnp.sum(held, axis=1, keepdims=True) * average).astype(BF)


def is_even():
    return lax.rem(lax.axis_index("mem"), 2) == 0


def boundary_kernel(blocks, x_ref, obs_ref, across_ref, partner_ref):
    first, last = rows_of((0, blocks - 1), blocks, x_ref, obs_ref)

    @pl.when(is_even())
    def _():
        across_ref[...] = first
        partner_ref[...] = last

    @pl.when(jnp.logical_not(is_even()))
    def _():
        across_ref[...] = last
        partner_ref[...] = first


def ordered(across_ref, partner_ref):
    across, partner = gram_of(across_ref[...]), gram_of(partner_ref[...])
    even = is_even()
    return jnp.where(even, across, partner), jnp.where(even, partner, across)


def finish(places, localized, members, out_ref):
    for place, transform, load in zip(places, transforms(localized, eye_of(128)), members):
        result = apply_to(transform, load())
        width = result.shape[1]
        out_ref[:, :, place * width : (place + 1) * width] = result.reshape(out_ref.shape[:2] + (width,))


def interior_kernel(
    blocks, x_ref, obs_ref, across_ref, partner_ref, inner_ref, part_ref, edge_ref
):
    first, last = ordered(across_ref, partner_ref)
    chosen = range(1, blocks - 1)
    rows = rows_of(chosen, blocks, x_ref, obs_ref)
    grams = [first] + [gram_of(r) for r in rows] + [last]
    part_ref[0] = grams[0] + localize * grams[1]
    part_ref[1] = grams[-1] + localize * grams[-2]
    localized = [grams[b] + localize * (grams[b - 1] + grams[b + 1]) for b in chosen]
    width = x_ref.shape[2] // blocks
    edge_ref[0] = members_of(x_ref, 0, width)
    edge_ref[1] = members_of(x_ref, blocks - 1, width)
    members = [lambda b=b: members_of(x_ref, b, width) for b in chosen]
    finish([b - 1 for b in chosen], localized, members, inner_ref)


def analysis_kernel(blocks, edge_ref, part_ref, across_ref, partner_ref, inner_ref, out_ref):
    width = edge_ref.shape[2]
    left, right = ordered(across_ref, partner_ref)
    localized = [part_ref[0] + localize * left, part_ref[1] + localize * right]
    out_ref[:, :, width : (blocks - 1) * width] = inner_ref[...]
    finish((0, blocks - 1), localized, [lambda: edge_ref[0], lambda: edge_ref[1]], out_ref)


VMEM = pl.BlockSpec(memory_space=pltpu.VMEM)


def call(kernel, out_shape, args, flops):
    outs = jax.tree.map(lambda _: VMEM, out_shape)
    moved = sum(a.size * a.dtype.itemsize for a in args)
    return pl.pallas_call(
        kernel,
        out_shape=out_shape,
        in_specs=[VMEM] * len(args),
        out_specs=outs,
        cost_estimate=pl.CostEstimate(flops=flops, bytes_accessed=moved, transcendentals=0),
        compiler_params=pltpu.CompilerParams(vmem_limit_bytes=40 * 2**20),
    )(*args)


def packed(obs_cell, obs_count, obs_value, obs_rinv):
    slot = lax.broadcasted_iota(jnp.int32, obs_cell.shape, 1)
    root = jnp.where(slot < obs_count[:, None], jnp.sqrt(obs_rinv), 0.0)
    return jnp.concatenate([obs_cell.astype(F32), obs_value, root], axis=0)


def analyse(arrived, obs, exchange):
    blocks, slots = obs.shape[0] // 3, obs.shape[1]
    kernel = lambda body: (lambda *refs: body(blocks, *refs))
    rows = jax.ShapeDtypeStruct((ROWS, slots), BF)
    across, partner = call(kernel(boundary_kernel), (rows, rows), (arrived, obs), 2 * 10**8)
    halo = exchange(across, partner)
    inner = jax.ShapeDtypeStruct(arrived.shape[:2] + (arrived.shape[2] // blocks * (blocks - 2),), BF)
    part = jax.ShapeDtypeStruct((2, ROWS, 128), F32)
    edge = jax.ShapeDtypeStruct((2, 128, arrived.shape[2] // blocks), BF)
    inner, part, edge = call(
        kernel(interior_kernel), (inner, part, edge), (arrived, obs, across, partner), 5 * 10**9
    )
    return call(
        kernel(analysis_kernel), jax.ShapeDtypeStruct(arrived.shape, BF), (edge, part) + halo + (inner,), 2 * 10**9
    )


def swap_boundaries(across, partner):
    count = lax.axis_size("mem")
    hops = [(i, (i + 1) % count) for i in range(1, count, 2)]
    cores = [(i, i + 1) for i in range(0, count, 2)]
    both_ways = lambda pairs: pairs + [(target, source) for source, target in pairs]
    return lax.ppermute(across, "mem", both_ways(hops)), lax.ppermute(partner, "mem", both_ways(cores))


def on_device(ensemble, obs_cell, obs_count, obs_value, obs_rinv):
    groups = lax.axis_size("mem")
    local, cells = ensemble.shape
    arrived = lax.all_to_all(ensemble, "mem", split_axis=1, concat_axis=1, tiled=True)
    arrived = arrived.reshape(local, groups, cells // groups).transpose(1, 0, 2)
    obs = packed(obs_cell[0], obs_count[0], obs_value[0], obs_rinv[0])
    outgoing = analyse(arrived, obs, swap_boundaries)
    outgoing = outgoing.transpose(1, 0, 2).reshape(local, cells)
    return lax.all_to_all(outgoing, "mem", split_axis=1, concat_axis=1, tiled=True)


def solution(mesh):
    placed = (
        P("mem", "blk"),
        P("blk", "mem", None),
        P("blk", "mem"),
        P("blk", "mem", None),
        P("blk", "mem", None),
    )
    return jax.shard_map(
        on_device, mesh=mesh, in_specs=placed, out_specs=P("mem", "blk"), check_vma=False
    )
```

```python
import jax
import jax.numpy as jnp
from jax import lax
from jax.experimental import pallas as pl
from jax.experimental.pallas import tpu as pltpu
from jax.sharding import PartitionSpec as P

NS_ITERS = 4
localize = 0.5
inflation = 1.1

BF = jnp.bfloat16
F32 = jnp.float32
ROWS = 136


def split(a):
    high = a.astype(BF)
    return high, (a - high.astype(F32)).astype(BF)


def left_of(a):
    high, low = split(a)
    return jnp.concatenate([high, low, high], axis=1)


def right_of(a):
    high, low = split(a)
    return jnp.concatenate([high, high, low], axis=0)


def dot(a, b):
    return jnp.dot(a, b, preferred_element_type=F32)


def members_of(x_ref, b, width):
    piece = x_ref[:, :, b * width : (b + 1) * width]
    return piece.reshape(piece.shape[0] * piece.shape[1], width)


def sample(members, cells):
    position = lax.broadcasted_iota(jnp.int32, (members.shape[1], cells.shape[1]), 0)
    return dot(members, jnp.where(position == cells, 1.0, 0.0).astype(BF))


def weigh(sampled, obs_value, root):
    size, slots = sampled.shape
    mean_at = jnp.sum(sampled, axis=0, keepdims=True) * (1.0 / size)
    line = lax.broadcasted_iota(jnp.int32, (ROWS - size, slots), 0)
    lower = jnp.where(line == 0, root * (obs_value - mean_at), 0.0)
    return jnp.concatenate([((sampled - mean_at) * root).astype(BF), lower.astype(BF)], axis=0)


def rows_of(chosen, blocks, x_ref, obs_ref):
    width = x_ref.shape[2] // blocks
    of_kind = lambda kind, b: obs_ref[kind * blocks + b : kind * blocks + b + 1]
    sampled = [sample(members_of(x_ref, b, width), of_kind(0, b).astype(jnp.int32)) for b in chosen]
    return [weigh(s, of_kind(1, b), of_kind(2, b)) for b, s in zip(chosen, sampled)]


def gram_of(rows):
    return lax.dot_general(rows, rows[:128], (((1,), (1,)), ((), ())), preferred_element_type=F32)


def eye_of(size):
    i = lax.broadcasted_iota(jnp.int32, (size, size), 0)
    j = lax.broadcasted_iota(jnp.int32, (size, size), 1)
    return jnp.where(i == j, 1.0, 0.0).astype(F32)


def transforms(localized, eye):
    size = eye.shape[0]
    systems = [g[:size] + (size - 1) / inflation * eye for g in localized]
    forcings = [g[size : size + 1] for g in localized]
    bounds = [
        jnp.max(jnp.sum(jnp.abs(a), axis=0, keepdims=True), axis=1, keepdims=True) for a in systems
    ]
    scales = [1.0 / b for b in bounds]
    squares = [dot(left_of(a), right_of(a)) for a in systems]
    y = [s * (1.5 * a - (0.5 * s) * q) for a, q, s in zip(systems, squares, scales)]
    z = [1.5 * eye - (0.5 * s) * a for a, s in zip(systems, scales)]
    for iteration in range(NS_ITERS - 1):
        u = [1.5 * eye - 0.5 * dot(left_of(a), right_of(b)) for a, b in zip(z, y)]
        if iteration < NS_ITERS - 2:
            both = [
                dot(jnp.concatenate([left_of(a), left_of(c)], axis=0), right_of(b))
                for a, c, b in zip(y, z, u)
            ]
            y = [a[:size] for a in both]
            z = [a[size:] for a in both]
        else:
            columns = [jnp.sum(eye * f, axis=1, keepdims=True) for f in forcings]
            early = [jnp.sum(a * c, axis=0, keepdims=True) for a, c in zip(z, columns)]
            inner = [jnp.sum(b * e, axis=1, keepdims=True) for b, e in zip(u, early)]
            z = [dot(left_of(a), right_of(b)) for a, b in zip(z, u)]
    out = []
    for a, i, s in zip(z, inner, scales):
        weights = jnp.sum(a * i, axis=0, keepdims=True) * s
        out.append(jnp.sqrt(s * (size - 1.0)) * a + weights - eye)
    return out


def apply_to(transform, members):
    size = transform.shape[0]
    high, low = split(transform)
    held = high.astype(F32) + low.astype(F32)
    line = lax.broadcasted_iota(jnp.int32, (16, 2 * size), 0)
    lane = lax.broadcasted_iota(jnp.int32, (16, 2 * size), 1)
    ones = jnp.where(jnp.logical_and(line == 0, lane < size), 1.0, 0.0).astype(BF)
    left = jnp.concatenate([jnp.concatenate([high, low], axis=1), ones], axis=0)
    product = dot(left, jnp.concatenate([members] * 2, axis=0))
    average = product[size : size + 1] * (1.0 / size)
    return (product[:size] - jnp.sum(held, axis=1, keepdims=True) * average).astype(BF)


def is_even():
    return lax.rem(lax.axis_index("mem"), 2) == 0


def boundary_kernel(blocks, x_ref, obs_ref, across_ref, partner_ref):
    first, last = rows_of((0, blocks - 1), blocks, x_ref, obs_ref)

    @pl.when(is_even())
    def _():
        across_ref[...] = first
        partner_ref[...] = last

    @pl.when(jnp.logical_not(is_even()))
    def _():
        across_ref[...] = last
        partner_ref[...] = first


def ordered(across_ref, partner_ref):
    across, partner = gram_of(across_ref[...]), gram_of(partner_ref[...])
    even = is_even()
    return jnp.where(even, across, partner), jnp.where(even, partner, across)


def finish(places, localized, members, out_ref):
    for place, transform, load in zip(places, transforms(localized, eye_of(128)), members):
        result = apply_to(transform, load())
        width = result.shape[1]
        out_ref[:, :, place * width : (place + 1) * width] = result.reshape(out_ref.shape[:2] + (width,))


def interior_kernel(
    blocks, x_ref, obs_ref, across_ref, partner_ref, inner_ref, part_ref, edge_ref
):
    first, last = ordered(across_ref, partner_ref)
    chosen = range(1, blocks - 1)
    rows = rows_of(chosen, blocks, x_ref, obs_ref)
    grams = [first] + [gram_of(r) for r in rows] + [last]
    part_ref[0] = grams[0] + localize * grams[1]
    part_ref[1] = grams[-1] + localize * grams[-2]
    localized = [grams[b] + localize * (grams[b - 1] + grams[b + 1]) for b in chosen]
    width = x_ref.shape[2] // blocks
    edge_ref[0] = members_of(x_ref, 0, width)
    edge_ref[1] = members_of(x_ref, blocks - 1, width)
    members = [lambda b=b: members_of(x_ref, b, width) for b in chosen]
    finish([b - 1 for b in chosen], localized, members, inner_ref)


def analysis_kernel(blocks, edge_ref, part_ref, across_ref, partner_ref, inner_ref, out_ref):
    width = edge_ref.shape[2]
    left, right = ordered(across_ref, partner_ref)
    localized = [part_ref[0] + localize * left, part_ref[1] + localize * right]
    out_ref[:, :, width : (blocks - 1) * width] = inner_ref[...]
    finish((0, blocks - 1), localized, [lambda: edge_ref[0], lambda: edge_ref[1]], out_ref)


VMEM = pl.BlockSpec(memory_space=pltpu.VMEM)


def call(kernel, out_shape, args, flops):
    outs = jax.tree.map(lambda _: VMEM, out_shape)
    moved = sum(a.size * a.dtype.itemsize for a in args)
    return pl.pallas_call(
        kernel,
        out_shape=out_shape,
        in_specs=[VMEM] * len(args),
        out_specs=outs,
        cost_estimate=pl.CostEstimate(flops=flops, bytes_accessed=moved, transcendentals=0),
        compiler_params=pltpu.CompilerParams(vmem_limit_bytes=40 * 2**20),
    )(*args)


def packed(obs_cell, obs_count, obs_value, obs_rinv):
    slot = lax.broadcasted_iota(jnp.int32, obs_cell.shape, 1)
    root = jnp.where(slot < obs_count[:, None], jnp.sqrt(obs_rinv), 0.0)
    return jnp.concatenate([obs_cell.astype(F32), obs_value, root], axis=0)


def analyse(arrived, obs, exchange):
    blocks, slots = obs.shape[0] // 3, obs.shape[1]
    kernel = lambda body: (lambda *refs: body(blocks, *refs))
    rows = jax.ShapeDtypeStruct((ROWS, slots), BF)
    across, partner = call(kernel(boundary_kernel), (rows, rows), (arrived, obs), 2 * 10**8)
    halo = exchange(across, partner)
    inner = jax.ShapeDtypeStruct(arrived.shape[:2] + (arrived.shape[2] // blocks * (blocks - 2),), BF)
    part = jax.ShapeDtypeStruct((2, ROWS, 128), F32)
    edge = jax.ShapeDtypeStruct((2, 128, arrived.shape[2] // blocks), BF)
    inner, part, edge = call(
        kernel(interior_kernel), (inner, part, edge), (arrived, obs, across, partner), 5 * 10**9
    )
    return call(
        kernel(analysis_kernel), jax.ShapeDtypeStruct(arrived.shape, BF), (edge, part) + halo + (inner,), 2 * 10**9
    )


def swap_boundaries(across, partner):
    count = lax.axis_size("mem")
    hops = [(i, (i + 1) % count) for i in range(1, count, 2)]
    cores = [(i, i + 1) for i in range(0, count, 2)]
    both_ways = lambda pairs: pairs + [(target, source) for source, target in pairs]
    return lax.ppermute(across, "mem", both_ways(hops)), lax.ppermute(partner, "mem", both_ways(cores))


def on_device(ensemble, obs_cell, obs_count, obs_value, obs_rinv):
    groups = lax.axis_size("mem")
    local, cells = ensemble.shape
    arrived = lax.all_to_all(ensemble, "mem", split_axis=1, concat_axis=1, tiled=True)
    arrived = arrived.reshape(local, groups, cells // groups).transpose(1, 0, 2)
    obs = packed(obs_cell[0], obs_count[0], obs_value[0], obs_rinv[0])
    outgoing = analyse(arrived, obs, swap_boundaries)
    outgoing = outgoing.transpose(1, 0, 2).reshape(local, cells)
    return lax.all_to_all(outgoing, "mem", split_axis=1, concat_axis=1, tiled=True)


def solution(mesh):
    placed = (
        P("mem", "blk"),
        P("blk", "mem", None),
        P("blk", "mem"),
        P("blk", "mem", None),
        P("blk", "mem", None),
    )
    return jax.shard_map(
        on_device, mesh=mesh, in_specs=placed, out_specs=P("mem", "blk"), check_vma=False
    )
```

```python
import jax
import jax.numpy as jnp
from jax import lax
from jax.experimental import pallas as pl
from jax.experimental.pallas import tpu as pltpu
from jax.sharding import PartitionSpec as P

NS_ITERS = 4
localize = 0.5
inflation = 1.1

BF = jnp.bfloat16
F32 = jnp.float32
ROWS = 136


def split(a):
    high = a.astype(BF)
    return high, (a - high.astype(F32)).astype(BF)


def left_of(a):
    high, low = split(a)
    return jnp.concatenate([high, low, high], axis=1)


def right_of(a):
    high, low = split(a)
    return jnp.concatenate([high, high, low], axis=0)


def dot(a, b):
    return jnp.dot(a, b, preferred_element_type=F32)


def members_of(x_ref, b, width):
    piece = x_ref[:, :, b * width : (b + 1) * width]
    return piece.reshape(piece.shape[0] * piece.shape[1], width)


def sample(members, cells):
    position = lax.broadcasted_iota(jnp.int32, (members.shape[1], cells.shape[1]), 0)
    return dot(members, jnp.where(position == cells, 1.0, 0.0).astype(BF))


def weigh(sampled, obs_value, root):
    size, slots = sampled.shape
    mean_at = jnp.sum(sampled, axis=0, keepdims=True) * (1.0 / size)
    line = lax.broadcasted_iota(jnp.int32, (ROWS - size, slots), 0)
    lower = jnp.where(line == 0, root * (obs_value - mean_at), 0.0)
    return jnp.concatenate([((sampled - mean_at) * root).astype(BF), lower.astype(BF)], axis=0)


def rows_of(chosen, blocks, x_ref, obs_ref):
    width = x_ref.shape[2] // blocks
    of_kind = lambda kind, b: obs_ref[kind * blocks + b : kind * blocks + b + 1]
    sampled = [sample(members_of(x_ref, b, width), of_kind(0, b).astype(jnp.int32)) for b in chosen]
    return [weigh(s, of_kind(1, b), of_kind(2, b)) for b, s in zip(chosen, sampled)]


def gram_of(rows):
    return lax.dot_general(rows, rows[:128], (((1,), (1,)), ((), ())), preferred_element_type=F32)


def eye_of(size):
    i = lax.broadcasted_iota(jnp.int32, (size, size), 0)
    j = lax.broadcasted_iota(jnp.int32, (size, size), 1)
    return jnp.where(i == j, 1.0, 0.0).astype(F32)


def transforms(localized, eye):
    size = eye.shape[0]
    systems = [g[:size] + (size - 1) / inflation * eye for g in localized]
    forcings = [g[size : size + 1] for g in localized]
    bounds = [
        jnp.max(jnp.sum(jnp.abs(a), axis=0, keepdims=True), axis=1, keepdims=True) for a in systems
    ]
    scales = [1.0 / b for b in bounds]
    squares = [dot(left_of(a), right_of(a)) for a in systems]
    y = [s * (1.5 * a - (0.5 * s) * q) for a, q, s in zip(systems, squares, scales)]
    z = [1.5 * eye - (0.5 * s) * a for a, s in zip(systems, scales)]
    for iteration in range(NS_ITERS - 1):
        u = [1.5 * eye - 0.5 * dot(left_of(a), right_of(b)) for a, b in zip(z, y)]
        if iteration < NS_ITERS - 2:
            both = [
                dot(jnp.concatenate([left_of(a), left_of(c)], axis=0), right_of(b))
                for a, c, b in zip(y, z, u)
            ]
            y = [a[:size] for a in both]
            z = [a[size:] for a in both]
        else:
            columns = [jnp.sum(eye * f, axis=1, keepdims=True) for f in forcings]
            early = [jnp.sum(a * c, axis=0, keepdims=True) for a, c in zip(z, columns)]
            inner = [jnp.sum(b * e, axis=1, keepdims=True) for b, e in zip(u, early)]
            z = [dot(left_of(a), right_of(b)) for a, b in zip(z, u)]
    out = []
    for a, i, s in zip(z, inner, scales):
        weights = jnp.sum(a * i, axis=0, keepdims=True) * s
        out.append(jnp.sqrt(s * (size - 1.0)) * a + weights - eye)
    return out


def apply_to(transform, members):
    size = transform.shape[0]
    high, low = split(transform)
    held = high.astype(F32) + low.astype(F32)
    line = lax.broadcasted_iota(jnp.int32, (8, 2 * size), 0)
    lane = lax.broadcasted_iota(jnp.int32, (8, 2 * size), 1)
    ones = jnp.where(jnp.logical_and(line == 0, lane < size), 1.0, 0.0).astype(BF)
    left = jnp.concatenate([jnp.concatenate([high, low], axis=1), ones], axis=0)
    product = dot(left, jnp.concatenate([members] * 2, axis=0))
    average = product[size : size + 1] * (1.0 / size)
    return (product[:size] - jnp.sum(held, axis=1, keepdims=True) * average).astype(BF)


def is_even():
    return lax.rem(lax.axis_index("mem"), 2) == 0


def boundary_kernel(blocks, x_ref, obs_ref, across_ref, partner_ref):
    first, last = rows_of((0, blocks - 1), blocks, x_ref, obs_ref)

    @pl.when(is_even())
    def _():
        across_ref[...] = first
        partner_ref[...] = last

    @pl.when(jnp.logical_not(is_even()))
    def _():
        across_ref[...] = last
        partner_ref[...] = first


def ordered(across_ref, partner_ref):
    across, partner = gram_of(across_ref[...]), gram_of(partner_ref[...])
    even = is_even()
    return jnp.where(even, across, partner), jnp.where(even, partner, across)


def finish(places, localized, members, out_ref):
    for place, transform, load in zip(places, transforms(localized, eye_of(128)), members):
        result = apply_to(transform, load())
        width = result.shape[1]
        out_ref[:, :, place * width : (place + 1) * width] = result.reshape(out_ref.shape[:2] + (width,))


def interior_kernel(
    blocks, x_ref, obs_ref, across_ref, partner_ref, inner_ref, part_ref, edge_ref
):
    first, last = ordered(across_ref, partner_ref)
    chosen = range(1, blocks - 1)
    rows = rows_of(chosen, blocks, x_ref, obs_ref)
    grams = [first] + [gram_of(r) for r in rows] + [last]
    part_ref[0] = grams[0] + localize * grams[1]
    part_ref[1] = grams[-1] + localize * grams[-2]
    localized = [grams[b] + localize * (grams[b - 1] + grams[b + 1]) for b in chosen]
    width = x_ref.shape[2] // blocks
    edge_ref[0] = members_of(x_ref, 0, width)
    edge_ref[1] = members_of(x_ref, blocks - 1, width)
    members = [lambda b=b: members_of(x_ref, b, width) for b in chosen]
    finish([b - 1 for b in chosen], localized, members, inner_ref)


def analysis_kernel(blocks, edge_ref, part_ref, across_ref, partner_ref, inner_ref, out_ref):
    width = edge_ref.shape[2]
    left, right = ordered(across_ref, partner_ref)
    localized = [part_ref[0] + localize * left, part_ref[1] + localize * right]
    out_ref[:, :, width : (blocks - 1) * width] = inner_ref[...]
    finish((0, blocks - 1), localized, [lambda: edge_ref[0], lambda: edge_ref[1]], out_ref)


VMEM = pl.BlockSpec(memory_space=pltpu.VMEM)


def call(kernel, out_shape, args, flops):
    outs = jax.tree.map(lambda _: VMEM, out_shape)
    moved = sum(a.size * a.dtype.itemsize for a in args)
    return pl.pallas_call(
        kernel,
        out_shape=out_shape,
        in_specs=[VMEM] * len(args),
        out_specs=outs,
        cost_estimate=pl.CostEstimate(flops=flops, bytes_accessed=moved, transcendentals=0),
        compiler_params=pltpu.CompilerParams(vmem_limit_bytes=40 * 2**20),
    )(*args)


def packed(obs_cell, obs_count, obs_value, obs_rinv):
    slot = lax.broadcasted_iota(jnp.int32, obs_cell.shape, 1)
    root = jnp.where(slot < obs_count[:, None], jnp.sqrt(obs_rinv), 0.0)
    return jnp.concatenate([obs_cell.astype(F32), obs_value, root], axis=0)


def analyse(arrived, obs, exchange):
    blocks, slots = obs.shape[0] // 3, obs.shape[1]
    kernel = lambda body: (lambda *refs: body(blocks, *refs))
    rows = jax.ShapeDtypeStruct((ROWS, slots), BF)
    across, partner = call(kernel(boundary_kernel), (rows, rows), (arrived, obs), 2 * 10**8)
    halo = exchange(across, partner)
    inner = jax.ShapeDtypeStruct(arrived.shape[:2] + (arrived.shape[2] // blocks * (blocks - 2),), BF)
    part = jax.ShapeDtypeStruct((2, ROWS, 128), F32)
    edge = jax.ShapeDtypeStruct((2, 128, arrived.shape[2] // blocks), BF)
    inner, part, edge = call(
        kernel(interior_kernel), (inner, part, edge), (arrived, obs, across, partner), 5 * 10**9
    )
    return call(
        kernel(analysis_kernel), jax.ShapeDtypeStruct(arrived.shape, BF), (edge, part) + halo + (inner,), 2 * 10**9
    )


def swap_boundaries(across, partner):
    count = lax.axis_size("mem")
    hops = [(i, (i + 1) % count) for i in range(1, count, 2)]
    cores = [(i, i + 1) for i in range(0, count, 2)]
    both_ways = lambda pairs: pairs + [(target, source) for source, target in pairs]
    return lax.ppermute(across, "mem", both_ways(hops)), lax.ppermute(partner, "mem", both_ways(cores))


def on_device(ensemble, obs_cell, obs_count, obs_value, obs_rinv):
    groups = lax.axis_size("mem")
    local, cells = ensemble.shape
    arrived = lax.all_to_all(ensemble, "mem", split_axis=1, concat_axis=1, tiled=True)
    arrived = arrived.reshape(local, groups, cells // groups).transpose(1, 0, 2)
    obs = packed(obs_cell[0], obs_count[0], obs_value[0], obs_rinv[0])
    outgoing = analyse(arrived, obs, swap_boundaries)
    outgoing = outgoing.transpose(1, 0, 2).reshape(local, cells)
    return lax.all_to_all(outgoing, "mem", split_axis=1, concat_axis=1, tiled=True)


def solution(mesh):
    placed = (
        P("mem", "blk"),
        P("blk", "mem", None),
        P("blk", "mem"),
        P("blk", "mem", None),
        P("blk", "mem", None),
    )
    return jax.shard_map(
        on_device, mesh=mesh, in_specs=placed, out_specs=P("mem", "blk"), check_vma=False
    )
```

```python
import jax
import jax.numpy as jnp
from jax import lax
from jax.experimental import pallas as pl
from jax.experimental.pallas import tpu as pltpu
from jax.sharding import PartitionSpec as P

NS_ITERS = 4
localize = 0.5
inflation = 1.1

BF = jnp.bfloat16
F32 = jnp.float32
ROWS = 136


def split(a):
    high = a.astype(BF)
    return high, (a - high.astype(F32)).astype(BF)


def left_of(a):
    high, low = split(a)
    return jnp.concatenate([high, low, high], axis=1)


def right_of(a):
    high, low = split(a)
    return jnp.concatenate([high, high, low], axis=0)


def dot(a, b):
    return jnp.dot(a, b, preferred_element_type=F32)


def members_of(x_ref, b, width):
    piece = x_ref[:, :, b * width : (b + 1) * width]
    return piece.reshape(piece.shape[0] * piece.shape[1], width)


def sample(members, cells):
    position = lax.broadcasted_iota(jnp.int32, (members.shape[1], cells.shape[1]), 0)
    return dot(members, jnp.where(position == cells, 1.0, 0.0).astype(BF))


def weigh(sampled, obs_value, root):
    size, slots = sampled.shape
    mean_at = jnp.sum(sampled, axis=0, keepdims=True) * (1.0 / size)
    line = lax.broadcasted_iota(jnp.int32, (ROWS - size, slots), 0)
    lower = jnp.where(line == 0, root * (obs_value - mean_at), 0.0)
    return jnp.concatenate([((sampled - mean_at) * root).astype(BF), lower.astype(BF)], axis=0)


def rows_of(chosen, blocks, x_ref, obs_ref):
    width = x_ref.shape[2] // blocks
    of_kind = lambda kind, b: obs_ref[kind * blocks + b : kind * blocks + b + 1]
    sampled = [sample(members_of(x_ref, b, width), of_kind(0, b).astype(jnp.int32)) for b in chosen]
    return [weigh(s, of_kind(1, b), of_kind(2, b)) for b, s in zip(chosen, sampled)]


def gram_of(rows):
    return lax.dot_general(rows, rows[:128], (((1,), (1,)), ((), ())), preferred_element_type=F32)


def eye_of(size):
    i = lax.broadcasted_iota(jnp.int32, (size, size), 0)
    j = lax.broadcasted_iota(jnp.int32, (size, size), 1)
    return jnp.where(i == j, 1.0, 0.0).astype(F32)


def transforms(localized, eye):
    size = eye.shape[0]
    systems = [g[:size] + (size - 1) / inflation * eye for g in localized]
    forcings = [g[size : size + 1] for g in localized]
    bounds = [
        jnp.max(jnp.sum(jnp.abs(a), axis=0, keepdims=True), axis=1, keepdims=True) for a in systems
    ]
    scales = [1.0 / b for b in bounds]
    squares = [dot(left_of(a), right_of(a)) for a in systems]
    y = [s * (1.5 * a - (0.5 * s) * q) for a, q, s in zip(systems, squares, scales)]
    z = [1.5 * eye - (0.5 * s) * a for a, s in zip(systems, scales)]
    for iteration in range(NS_ITERS - 1):
        u = [1.5 * eye - 0.5 * dot(left_of(a), right_of(b)) for a, b in zip(z, y)]
        if iteration < NS_ITERS - 2:
            both = [
                dot(jnp.concatenate([left_of(a), left_of(c)], axis=0), right_of(b))
                for a, c, b in zip(y, z, u)
            ]
            y = [a[:size] for a in both]
            z = [a[size:] for a in both]
        else:
            columns = [jnp.sum(eye * f, axis=1, keepdims=True) for f in forcings]
            early = [jnp.sum(a * c, axis=0, keepdims=True) for a, c in zip(z, columns)]
            inner = [jnp.sum(b * e, axis=1, keepdims=True) for b, e in zip(u, early)]
            z = [dot(left_of(a), right_of(b)) for a, b in zip(z, u)]
    out = []
    for a, i, s in zip(z, inner, scales):
        weights = jnp.sum(a * i, axis=0, keepdims=True) * s
        out.append(jnp.sqrt(s * (size - 1.0)) * a + weights - eye)
    return out


def apply_to(transform, members):
    size = transform.shape[0]
    high, low = split(transform)
    held = high.astype(F32) + low.astype(F32)
    line = lax.broadcasted_iota(jnp.int32, (16, 2 * size), 0)
    lane = lax.broadcasted_iota(jnp.int32, (16, 2 * size), 1)
    ones = jnp.where(jnp.logical_and(line == 0, lane < size), 1.0, 0.0).astype(BF)
    left = jnp.concatenate([jnp.concatenate([high, low], axis=1), ones], axis=0)
    product = dot(left, jnp.concatenate([members] * 2, axis=0))
    average = product[size : size + 1] * (1.0 / size)
    return (product[:size] - jnp.sum(held, axis=1, keepdims=True) * average).astype(BF)


def is_even():
    return lax.rem(lax.axis_index("mem"), 2) == 0


def boundary_kernel(blocks, x_ref, obs_ref, across_ref, partner_ref):
    first, last = rows_of((0, blocks - 1), blocks, x_ref, obs_ref)

    @pl.when(is_even())
    def _():
        across_ref[...] = first
        partner_ref[...] = last

    @pl.when(jnp.logical_not(is_even()))
    def _():
        across_ref[...] = last
        partner_ref[...] = first


def ordered(across_ref, partner_ref):
    across, partner = gram_of(across_ref[...]), gram_of(partner_ref[...])
    even = is_even()
    return jnp.where(even, across, partner), jnp.where(even, partner, across)


def finish(places, localized, members, out_ref):
    for place, transform, load in zip(places, transforms(localized, eye_of(128)), members):
        result = apply_to(transform, load())
        width = result.shape[1]
        out_ref[:, :, place * width : (place + 1) * width] = result.reshape(out_ref.shape[:2] + (width,))


def interior_kernel(
    blocks, x_ref, obs_ref, across_ref, partner_ref, inner_ref, part_ref, edge_ref
):
    first, last = ordered(across_ref, partner_ref)
    chosen = range(1, blocks - 1)
    rows = rows_of(chosen, blocks, x_ref, obs_ref)
    grams = [first] + [gram_of(r) for r in rows] + [last]
    part_ref[0] = grams[0] + localize * grams[1]
    part_ref[1] = grams[-1] + localize * grams[-2]
    localized = [grams[b] + localize * (grams[b - 1] + grams[b + 1]) for b in chosen]
    width = x_ref.shape[2] // blocks
    edge_ref[0] = members_of(x_ref, 0, width)
    edge_ref[1] = members_of(x_ref, blocks - 1, width)
    members = [lambda b=b: members_of(x_ref, b, width) for b in chosen]
    finish([b - 1 for b in chosen], localized, members, inner_ref)


def analysis_kernel(blocks, edge_ref, part_ref, across_ref, partner_ref, inner_ref, out_ref):
    width = edge_ref.shape[2]
    left, right = ordered(across_ref, partner_ref)
    localized = [part_ref[0] + localize * left, part_ref[1] + localize * right]
    finish((0, blocks - 1), localized, [lambda: edge_ref[0], lambda: edge_ref[1]], out_ref)
    out_ref[:, :, width : (blocks - 1) * width] = inner_ref[...]


VMEM = pl.BlockSpec(memory_space=pltpu.VMEM)


def call(kernel, out_shape, args, flops):
    outs = jax.tree.map(lambda _: VMEM, out_shape)
    moved = sum(a.size * a.dtype.itemsize for a in args)
    return pl.pallas_call(
        kernel,
        out_shape=out_shape,
        in_specs=[VMEM] * len(args),
        out_specs=outs,
        cost_estimate=pl.CostEstimate(flops=flops, bytes_accessed=moved, transcendentals=0),
        compiler_params=pltpu.CompilerParams(vmem_limit_bytes=40 * 2**20),
    )(*args)


def packed(obs_cell, obs_count, obs_value, obs_rinv):
    slot = lax.broadcasted_iota(jnp.int32, obs_cell.shape, 1)
    root = jnp.where(slot < obs_count[:, None], jnp.sqrt(obs_rinv), 0.0)
    return jnp.concatenate([obs_cell.astype(F32), obs_value, root], axis=0)


def analyse(arrived, obs, exchange):
    blocks, slots = obs.shape[0] // 3, obs.shape[1]
    kernel = lambda body: (lambda *refs: body(blocks, *refs))
    rows = jax.ShapeDtypeStruct((ROWS, slots), BF)
    across, partner = call(kernel(boundary_kernel), (rows, rows), (arrived, obs), 2 * 10**8)
    halo = exchange(across, partner)
    inner = jax.ShapeDtypeStruct(arrived.shape[:2] + (arrived.shape[2] // blocks * (blocks - 2),), BF)
    part = jax.ShapeDtypeStruct((2, ROWS, 128), F32)
    edge = jax.ShapeDtypeStruct((2, 128, arrived.shape[2] // blocks), BF)
    inner, part, edge = call(
        kernel(interior_kernel), (inner, part, edge), (arrived, obs, across, partner), 5 * 10**9
    )
    return call(
        kernel(analysis_kernel), jax.ShapeDtypeStruct(arrived.shape, BF), (edge, part) + halo + (inner,), 2 * 10**9
    )


def swap_boundaries(across, partner):
    count = lax.axis_size("mem")
    hops = [(i, (i + 1) % count) for i in range(1, count, 2)]
    cores = [(i, i + 1) for i in range(0, count, 2)]
    both_ways = lambda pairs: pairs + [(target, source) for source, target in pairs]
    return lax.ppermute(across, "mem", both_ways(hops)), lax.ppermute(partner, "mem", both_ways(cores))


def on_device(ensemble, obs_cell, obs_count, obs_value, obs_rinv):
    groups = lax.axis_size("mem")
    local, cells = ensemble.shape
    arrived = lax.all_to_all(ensemble, "mem", split_axis=1, concat_axis=1, tiled=True)
    arrived = arrived.reshape(local, groups, cells // groups).transpose(1, 0, 2)
    obs = packed(obs_cell[0], obs_count[0], obs_value[0], obs_rinv[0])
    outgoing = analyse(arrived, obs, swap_boundaries)
    outgoing = outgoing.transpose(1, 0, 2).reshape(local, cells)
    return lax.all_to_all(outgoing, "mem", split_axis=1, concat_axis=1, tiled=True)


def solution(mesh):
    placed = (
        P("mem", "blk"),
        P("blk", "mem", None),
        P("blk", "mem"),
        P("blk", "mem", None),
        P("blk", "mem", None),
    )
    return jax.shard_map(
        on_device, mesh=mesh, in_specs=placed, out_specs=P("mem", "blk"), check_vma=False
    )
```
